32 devices in a mesh: wide: 8 (over z, y), narrow: 4 (over x, core).
Axes of the slice: x: 2, y: 2, z: 4, core: 2. Of those that a mesh axis runs over, the one named last changes fastest.
Arguments:
- density_blocks: float32 [768, 128, 128], P(('wide', 'narrow')), may hold values from -0.4 to 0.4
- block_groups: int32 [768, 2], P(('wide', 'narrow')), may hold values from 0 to 63
- block_brick: int32 [768], P(('wide', 'narrow')), may hold values from 0 to 8191, as said below
- orbital_freq: float32 [3, 8192], replicated, may hold values from 0.1 to 2
- orbital_phase: float32 [3, 8192], replicated, may hold values from -3.140625 to 3.140625
- core_density: float32 [8, 1024, 1024], P('wide', None, 'narrow'), may hold values from 0.2 to 2
Outputs:
- xc_spectrum: float32 [8, 2, 1024, 512], P('wide', None, 'narrow')
The draws below stay inside these ranges and needn't reach their ends.
Inputs may be any that keep to these rules, and one draw needn't show every extreme that they name: `block_brick`: every block stored on the device of narrow index n has its brick within the columns n * 1024 / 4 to (n + 1) * 1024 / 4 - 1 of the grid. The blocks of one device have at most 6 bricks, counted with repeats, in the planes of any one index of wide, and some device has exactly 6.
All inputs are finite; a program needn't handle non-finite values.
Results may differ from the reference program's by a relative error of at most 0.0003.
Values sent between devices are 32-bit elements; how exact they have to be, the bound alone decides.
No kernel may reach another device: no remote copies, remote signals or barrier semaphores. Data moves between devices by JAX's collectives and lax.ppermute only.
A program may use at most 64 MiB of HBM per device.

```python
import math
import jax
import jax.numpy as jnp
from jax import lax

NX = 1024
NY = 1024
GRP = 128
BY = 32
BX = 32
NGRP = 64
BLK_DEV = 24
Z_DEV = 1
NORB = 8192
NZ = 8
NBLK = 768
N_WIDE = 8
N_NARROW = 4


def draw_block_brick(key, part):
    base_key = jax.random.fold_in(key, 11)
    row_keys = jax.random.split(base_key, N_NARROW)
    profile = jnp.array([2 * BLK_DEV, BLK_DEV, BLK_DEV // 2, BLK_DEV // 2], jnp.int32)
    row_loads = jnp.tile(profile, N_WIDE // 4)
    column_bricks = NX // N_NARROW // BX

    def one_row(row_key, row_index):
        keys_four = jax.random.split(row_key, 4)
        home_order = jax.random.permutation(keys_four[0], N_WIDE)
        home_loads = jnp.zeros((N_WIDE,), jnp.int32).at[home_order].set(row_loads)
        bounds = jnp.cumsum(home_loads)
        positions = jnp.arange(N_WIDE * BLK_DEV, dtype=jnp.int32)
        home_index = jnp.searchsorted(bounds, positions, side='right').astype(jnp.int32)
        total = N_WIDE * BLK_DEV
        plane_index = home_index * Z_DEV + jax.random.randint(keys_four[1], (total,), 0, Z_DEV)
        row_block = jax.random.randint(keys_four[2], (total,), 0, NY // BY)
        column_block = row_index * column_bricks + jax.random.randint(keys_four[3], (total,), 0, column_bricks)
        brick_ids = (plane_index * (NY // BY) + row_block) * (NX // BX) + column_block
        return brick_ids.reshape(BLK_DEV, N_WIDE).T
    row_bricks = jax.vmap(one_row)(row_keys, jnp.arange(N_NARROW, dtype=jnp.int32))
    return jnp.transpose(row_bricks, (1, 0, 2)).reshape(-1).astype(jnp.int32)


def set_ends(drawn, own_key, least, largest):
    index_at = [jax.random.randint(jax.random.fold_in(own_key, axis), (), 0, length) for axis, length in enumerate(drawn.shape)]
    main_axis = drawn.shape.index(max(drawn.shape))
    next_to = index_at[:main_axis] + [(index_at[main_axis] + 1) % drawn.shape[main_axis]] + index_at[main_axis + 1:]
    return drawn.at[tuple(index_at)].set(least).at[tuple(next_to)].set(largest)


def level_of(rng, extent, cuts, smallest, top_value):
    factor_of = 1.0
    for axis_at, blocks in cuts:
        heights = jax.random.uniform(jax.random.fold_in(jax.random.fold_in(rng, 6), axis_at), (blocks,), jnp.float32, smallest / len(cuts), top_value / len(cuts))
        factor_of = factor_of * jnp.repeat(jnp.exp(heights), extent[axis_at] // blocks).reshape((-1,) + (1,) * (len(extent) - 1 - axis_at))
    return factor_of


def scatter_about(stream_key, extent, scale, reach, shards=(), kind=jnp.bfloat16):
    factor_of = level_of(stream_key, extent, shards, -0.22, 0.18) if shards else 1.0
    entries = jax.random.normal(stream_key, extent, jnp.float32) * scale * factor_of
    return jnp.minimum(jnp.maximum(entries, -reach), reach).astype(kind)


def setup_inputs(seed: int = 0) -> dict:
    seeds = jax.random.split(jax.random.key(seed), 7)
    density_blocks = scatter_about(seeds[0], (NBLK, GRP, GRP), 0.06, 0.4, ((0, 32),), jnp.float32)
    block_groups = set_ends(jax.random.randint(seeds[1], (NBLK, 2), 0, NGRP), jax.random.fold_in(seeds[1], 1), 0, NGRP - 1).astype(jnp.int32)
    block_brick = draw_block_brick(jax.random.fold_in(seeds[6], 71), 0)
    orbital_freq = jnp.clip(jax.random.uniform(seeds[3], (3, NORB), jnp.float32, 0.1, 2.0), 0.1, 2.0)
    orbital_phase = jnp.clip(jax.random.uniform(seeds[4], (3, NORB), jnp.float32, -3.140625, 3.140625), -3.140625, 3.140625)
    core_density = jnp.clip(jnp.exp(math.log(2.0) - 2.3025851 * jax.random.uniform(seeds[5], (NZ, NY, NX), jnp.float32) ** level_of(seeds[5], (NZ, NY, NX), ((0, 8), (2, 4)), -0.2, 0.2)), 0.2, 2.0)
    return {"density_blocks": density_blocks, "block_groups": block_groups, "block_brick": block_brick, "orbital_freq": orbital_freq, "orbital_phase": orbital_phase, "core_density": core_density}


energy_coef = -0.75 * (3.0 / math.pi) ** (1.0 / 3.0)

def brick_pieces(blocks, group_pairs, brick_ids, orbital_freq, orbital_phase):
    row_bricks = NX // BX
    col_bricks = NY // BY
    column_block = brick_ids % row_bricks
    remainder = brick_ids // row_bricks
    row_block = remainder % col_bricks
    plane_index = remainder // col_bricks
    freq_groups = orbital_freq.reshape(3, -1, GRP)
    shift_groups = orbital_phase.reshape(3, -1, GRP)
    y_cells = (row_block * BY)[:, None] + jnp.arange(BY, dtype=jnp.int32)[None, :]
    x_cells = (column_block * BX)[:, None] + jnp.arange(BX, dtype=jnp.int32)[None, :]

    def orbital_values(group_ids):
        frequency = jnp.take(freq_groups, group_ids, axis=1)
        phase_shift = jnp.take(shift_groups, group_ids, axis=1)
        along_y = jnp.cos(y_cells.astype(jnp.float32)[:, :, None] * frequency[1][:, None, :] + phase_shift[1][:, None, :])
        along_x = jnp.cos(x_cells.astype(jnp.float32)[:, :, None] * frequency[0][:, None, :] + phase_shift[0][:, None, :])
        along_z = jnp.cos(plane_index.astype(jnp.float32)[:, None] * frequency[2] + phase_shift[2])
        orbital_table = along_y[:, :, None, :] * along_x[:, None, :, :] * along_z[:, None, None, :]
        return orbital_table.reshape(group_ids.shape[0], BY * BX, GRP)
    left_values = orbital_values(group_pairs[:, 0])
    right_values = orbital_values(group_pairs[:, 1])
    mixed_rows = jnp.einsum('sci,sij->scj', left_values, blocks, precision=lax.Precision.HIGHEST, preferred_element_type=jnp.float32)
    return lax.optimization_barrier(jnp.sum(mixed_rows * right_values, axis=2))

def reference(density_blocks, block_groups, block_brick, orbital_freq, orbital_phase, core_density):
    step_size = math.gcd(BLK_DEV, 8)
    blocks = density_blocks.reshape(-1, step_size, GRP, GRP)
    group_sets = block_groups.reshape(-1, step_size, 2)
    brick_sets = block_brick.reshape(-1, step_size)

    def one_batch(inputs):
        return brick_pieces(inputs[0], inputs[1], inputs[2], orbital_freq, orbital_phase)
    pieces = lax.map(one_batch, (blocks, group_sets, brick_sets)).reshape(-1, BY * BX)
    brick_total = NZ * (NY // BY) * (NX // BX)
    valence = jnp.zeros((brick_total, BY * BX), jnp.float32).at[block_brick].add(pieces)
    valence = valence.reshape(NZ, NY // BY, NX // BX, BY, BX).transpose(0, 1, 3, 2, 4).reshape(NZ, NY, NX)
    rho_total = core_density + valence
    energy = energy_coef * (rho_total * jnp.cbrt(rho_total) - core_density * jnp.cbrt(core_density))
    half_x = jnp.fft.rfft(energy, axis=2)[:, :, :NX // 2]
    spectrum = jnp.fft.fft(half_x, axis=1) / math.sqrt(NX * NY)
    stacked = jnp.stack([jnp.real(spectrum), jnp.imag(spectrum)], axis=1)
    return stacked.astype(jnp.float32)
```

```python
import functools
import math

import jax
import jax.numpy as jnp
from jax import lax
from jax.experimental import pallas as pl
from jax.experimental.pallas import tpu as pltpu
from jax.sharding import PartitionSpec as P

NX = 1024
NY = 1024
GRP = 128
BY = 32
BX = 32
LANES = 128
SUB = 8

f32 = jnp.float32
bf16 = jnp.bfloat16
i32 = jnp.int32

energy_coef = -0.75 * (3.0 / math.pi) ** (1.0 / 3.0)

COS_FIT = (0.999999989, -0.499999891, 0.0416664892, -0.00138878036, 2.47698836e-05, -2.70790308e-07, 1.72450917e-09)
SIN_FIT = (0.999999999, -0.166666659, 0.00833332129, -0.000198405341, 2.753585e-06, -2.47288117e-08, 1.36130988e-10)
TURN_HI = 6.28125
TURN_LO = 2.0 * math.pi - TURN_HI


def horner(w, fit):
    total = jnp.full_like(w, fit[-1])
    for term in fit[-2::-1]:
        total = total * w + term
    return total


def cos_any(angle):
    turns = jnp.floor(angle * (0.5 / math.pi) + 0.5)
    r = (angle - turns * TURN_HI) - turns * TURN_LO
    return horner(r * r, COS_FIT)


def cos_sin_turn(step, length):
    r = (step - length // 2).astype(f32) * (2.0 * math.pi / length)
    w = r * r
    return -horner(w, COS_FIT), -(r * horner(w, SIN_FIT))


def split(value):
    high = value.astype(bf16)
    return high, (value - high.astype(f32)).astype(bf16)


def dot3(lhs_high, lhs_low, rhs_high, rhs_low):
    dot = functools.partial(jnp.dot, preferred_element_type=f32)
    return dot(lhs_high, rhs_high) + dot(lhs_low, rhs_high) + dot(lhs_high, rhs_low)


def pieces_kernel(
    steps, per_step, slots, planes, groups_ref, brick_ref, blocks_ref, freq_ref, phase_ref,
    send_ref, count_ref, left_ref, right_ref, mixed_ref,
):
    row_bricks = NX // BX
    col_bricks = NY // BY
    wide_size = send_ref.shape[0]
    narrow_size = lax.axis_size("narrow")
    narrow = lax.axis_index("narrow")
    column_bricks = row_bricks // narrow_size
    flip = (2 * narrow < narrow_size).astype(i32)
    step = pl.program_id(0)
    lane = lax.broadcasted_iota(i32, (SUB, LANES), 1)
    row = lax.broadcasted_iota(i32, (BY, GRP), 0)

    @pl.when(step == 0)
    def _():
        zero = jnp.zeros((slots * SUB, LANES), f32)
        none = jnp.full((SUB, LANES), -1.0, f32)
        for w in range(wide_size):
            send_ref[w, : slots * SUB, :] = zero
            send_ref[w, slots * SUB :, :] = none
            count_ref[w] = 0

    def one_block(k, carry):
        b = step * per_step + k
        q = brick_ref[b]
        xb = q % row_bricks
        yb = (q // row_bricks) % col_bricks
        zb = q // (row_bricks * col_bricks)
        home = zb // planes
        local = ((zb % planes) * col_bricks + yb) * column_bricks + (xb - narrow * column_bricks)
        rank = count_ref[home]
        count_ref[home] = rank + 1

        ys = (yb * BY + row).astype(f32)
        xs = (xb * BX + jnp.where(flip == 1, BX - 1 - row, row)).astype(f32)
        zs = zb.astype(f32)

        def factors(side):
            group = groups_ref[side, b]
            at = pl.ds(pl.multiple_of(group * GRP, GRP), GRP)
            freq = freq_ref[:, at]
            phase = phase_ref[:, at]
            along_x = cos_any(xs * freq[0:1] + phase[0:1])
            along_y = cos_any(ys * freq[1:2] + phase[1:2])
            along_z = cos_any(jnp.broadcast_to(zs * freq[2:3] + phase[2:3], (SUB, GRP)))
            return along_x, along_y * along_z[0:1]

        left_x, left_y = factors(0)
        right_x, right_y = factors(1)
        left = (left_x[None, :, None, :] * left_y.reshape(BY // SUB, 1, SUB, GRP)).reshape(BY * BX, GRP)
        high, low = split(left)
        left_ref[:, :GRP] = high
        left_ref[:, GRP:] = low
        d_high, d_low = split(blocks_ref[k])
        right_ref[:GRP, :GRP] = d_high
        right_ref[GRP:, :GRP] = d_high
        right_ref[:GRP, GRP:] = d_low
        right_ref[GRP:, GRP:] = d_low
        mixed_ref[...] = jnp.dot(left_ref[...], right_ref[...], preferred_element_type=f32)

        def merge(value, bit):
            count = value.shape[0]
            pair = value.reshape(count // 2, 2, SUB, LANES)
            first, second = pair[:, 0], pair[:, 1]
            odd = (lane & bit) != 0
            keep = jnp.where(odd, second, first)
            move = jnp.where(odd, first, second)
            moved = pltpu.roll(move.reshape(-1, LANES), bit, 1).reshape(count // 2, SUB, LANES)
            return keep + moved

        parts = []
        for chunk in range(8):
            rows = pl.ds(chunk * 128, 128)
            mixed = mixed_ref[rows, :GRP] + mixed_ref[rows, GRP:]
            g, x0 = chunk // 2, (chunk % 2) * 16
            right = right_x[x0 : x0 + 16][:, None, :] * right_y[g * SUB : (g + 1) * SUB][None]
            value = mixed.reshape(16, SUB, GRP) * right
            for bit in (1, 2, 4, 8):
                value = merge(value, bit)
            parts.append(value)
        value = jnp.concatenate(parts, axis=0)
        for bit in (16, 32, 64):
            value = merge(value, bit)
        at = pl.multiple_of(rank * SUB, SUB)
        send_ref[home, pl.ds(at, SUB), :] = value[0]
        send_ref[home, pl.ds(slots * SUB + rank, 1), :] = jnp.full((1, LANES), 1.0, f32) * local.astype(f32)
        return carry

    lax.fori_loop(0, per_step, one_block, 0)


def make_pieces(blocks, groups, bricks, freq, phase, wide_size, slots, planes):
    count = blocks.shape[0]
    per_step = math.gcd(count, 8)
    steps = count // per_step
    rows = slots * SUB + SUB
    return pl.pallas_call(
        functools.partial(pieces_kernel, steps, per_step, slots, planes),
        grid=(steps,),
        in_specs=[
            pl.BlockSpec(memory_space=pltpu.SMEM),
            pl.BlockSpec(memory_space=pltpu.SMEM),
            pl.BlockSpec((per_step, GRP, GRP), lambda s: (s, 0, 0)),
            pl.BlockSpec(freq.shape, lambda s: (0, 0)),
            pl.BlockSpec(phase.shape, lambda s: (0, 0)),
        ],
        out_specs=pl.BlockSpec((wide_size, rows, LANES), lambda s: (0, 0, 0)),
        out_shape=jax.ShapeDtypeStruct((wide_size, rows, LANES), f32),
        scratch_shapes=[
            pltpu.SMEM((wide_size,), i32),
            pltpu.VMEM((BY * BX, 2 * GRP), bf16),
            pltpu.VMEM((2 * GRP, 2 * GRP), bf16),
            pltpu.VMEM((BY * BX, 2 * GRP), f32),
        ],
        name="pieces",
    )(groups.T, bricks, blocks, freq, phase)


def energy_kernel(slots, ids_ref, got_ref, core_ref, out_ref, first_ref, valence_ref, cells_ref):
    wide_size = got_ref.shape[0]
    total = wide_size * slots
    narrow_size = lax.axis_size("narrow")
    narrow = lax.axis_index("narrow")
    column_bricks = core_ref.shape[1] // BX
    tiles = LANES // BX
    flip = 2 * narrow < narrow_size
    lane = lax.broadcasted_iota(i32, (SUB, LANES), 1)
    group = lane // BX

    for s in range(total - 1, -1, -1):
        first_ref[jnp.maximum(ids_ref[s], 0)] = s
    for s in range(total):
        valence_ref[s * SUB : (s + 1) * SUB, :] = got_ref[s // slots, (s % slots) * SUB : (s % slots + 1) * SUB, :]
    head = jnp.full((SUB, LANES), -1.0, f32)
    sub = lax.broadcasted_iota(i32, (SUB, LANES), 0)
    for s in range(total):
        brick = ids_ref[s]
        at = jnp.maximum(brick, 0)
        valid = brick >= 0
        owner = first_ref[at]

        @pl.when(owner != s)
        def _():
            rows = pl.ds(pl.multiple_of(owner * SUB, SUB), SUB)
            valence_ref[rows, :] = valence_ref[rows, :] + got_ref[s // slots, (s % slots) * SUB : (s % slots + 1) * SUB, :]

        column = at % column_bricks
        placed = jnp.where(flip, at - column + (column_bricks - 1 - column), at)
        mark = jnp.where(owner == s, placed, -1).astype(f32)
        head = jnp.where((lane == s % LANES) & (sub == s // LANES), mark, head)
        y0 = pl.multiple_of((at // column_bricks) * BY, BY)
        lanes = pl.ds(pl.multiple_of((column // tiles) * LANES, LANES), LANES)
        block = core_ref[pl.ds(y0, BY), lanes]
        block = pltpu.roll(block, ((tiles - column % tiles) % tiles) * BX, 1)
        value = block[0:SUB]
        for g in range(1, tiles):
            moved = pltpu.roll(block[g * SUB : (g + 1) * SUB], g * BX, 1)
            value = jnp.where(group == g, moved, value)
        cells_ref[s * SUB : (s + 1) * SUB, :] = value

    core = cells_ref[...]
    source = lax.broadcasted_iota(i32, (LANES, LANES), 0)
    target = lax.broadcasted_iota(i32, (LANES, LANES), 1)
    wanted = jnp.where(flip, (target // BX) * BX + (BX - 1 - target % BX), target)
    shuffle = (source == wanted).astype(bf16)
    high = core.astype(bf16)
    rest = core - high.astype(f32)
    mid = rest.astype(bf16)
    low = (rest - mid.astype(f32)).astype(bf16)
    dot = functools.partial(jnp.dot, preferred_element_type=f32)
    core = (dot(low, shuffle) + dot(mid, shuffle)) + dot(high, shuffle)

    def four_thirds(value):
        size = jnp.maximum(jnp.abs(value), 1e-30)
        inverse = jnp.exp2(jnp.log2(size) * (-1.0 / 3.0))
        inverse = inverse * (4.0 - size * (inverse * inverse * inverse)) * (1.0 / 3.0)
        return size * (size * (inverse * inverse))

    rho = core + valence_ref[...]
    out_ref[: total * SUB, :] = energy_coef * (four_thirds(rho) - four_thirds(core))
    out_ref[total * SUB :, :] = head


def make_energy(got, ids, core, slots):
    wide_size = got.shape[0]
    total = wide_size * slots
    bricks = (core.shape[0] // BY) * (core.shape[1] // BX)
    return pl.pallas_call(
        functools.partial(energy_kernel, slots),
        in_specs=[
            pl.BlockSpec(memory_space=pltpu.SMEM),
            pl.BlockSpec(memory_space=pltpu.VMEM),
            pl.BlockSpec(memory_space=pltpu.VMEM),
        ],
        out_specs=pl.BlockSpec(memory_space=pltpu.VMEM),
        out_shape=jax.ShapeDtypeStruct(((total + 1) * SUB, LANES), f32),
        scratch_shapes=[
            pltpu.SMEM((bricks,), i32),
            pltpu.VMEM((total * SUB, LANES), f32),
            pltpu.VMEM((total * SUB, LANES), f32),
        ],
        name="energy",
    )(ids, got, core)


def tables_kernel(wy_high, wy_low, wx_high, wx_low):
    rows_all = NY // lax.axis_size("narrow")
    narrow = lax.axis_index("narrow")
    half = rows_all // 2
    depth = NY // 2
    lane = lax.broadcasted_iota(i32, (half, LANES), 1)
    row = lax.broadcasted_iota(i32, (half, LANES), 0)
    for p in range(2):
        wave = rows_all * narrow + 2 * row + p
        base_cos, base_sin = cos_sin_turn((wave * lane) % NY, NY)
        for t in range(depth // LANES):
            jump_cos, jump_sin = cos_sin_turn((wave[:SUB] * (t * LANES)) % NY, NY)
            jump_cos = jnp.concatenate([jump_cos] * (half // SUB), axis=0)
            jump_sin = jnp.concatenate([jump_sin] * (half // SUB), axis=0)
            at = slice(t * LANES, (t + 1) * LANES)
            for part, value in (
                (0, base_cos * jump_cos - base_sin * jump_sin),
                (1, -(base_sin * jump_cos + base_cos * jump_sin)),
            ):
                rows = slice(p * rows_all + part * half, p * rows_all + (part + 1) * half)
                wy_high[rows, at], wy_low[rows, at] = split(value)
    depth = NX // 2
    lane = lax.broadcasted_iota(i32, (depth, LANES), 1)
    place = 2 * lax.broadcasted_iota(i32, (depth, LANES), 0) + 1
    base_cos, base_sin = cos_sin_turn((place * lane) % (2 * NX), 2 * NX)
    for t in range(NX // 2 // LANES):
        jump_cos, jump_sin = cos_sin_turn((place[:SUB] * (t * LANES)) % (2 * NX), 2 * NX)
        jump_cos = jnp.concatenate([jump_cos] * (depth // SUB), axis=0)
        jump_sin = jnp.concatenate([jump_sin] * (depth // SUB), axis=0)
        at = slice(t * LANES, (t + 1) * LANES)
        for part, value in (
            (0, base_cos * jump_cos - base_sin * jump_sin),
            (1, base_sin * jump_cos + base_cos * jump_sin),
        ):
            rows = slice(part * depth, (part + 1) * depth)
            wx_high[rows, at], wx_low[rows, at] = split(value)


def make_tables(narrow_size):
    rows_all = NY // narrow_size
    y_shape = jax.ShapeDtypeStruct((2 * rows_all, NY // 2), bf16)
    x_shape = jax.ShapeDtypeStruct((NX, NX // 2), bf16)
    vmem = pl.BlockSpec(memory_space=pltpu.VMEM)
    return pl.pallas_call(
        tables_kernel,
        out_specs=[vmem] * 4,
        out_shape=[y_shape, y_shape, x_shape, x_shape],
        name="tables",
    )()


def along_y(total, ids_ref, bricks_ref, wy_high, wy_low, plane_ref, out_ref):
    columns = plane_ref.shape[1]
    column_bricks = columns // BX
    tiles = LANES // BX
    lane = lax.broadcasted_iota(i32, (SUB, LANES), 1)
    group = lane // BX
    plane_ref[...] = jnp.zeros(plane_ref.shape, f32)
    for s in range(total):
        brick = ids_ref[s]
        valid = brick >= 0
        at = jnp.maximum(brick, 0)
        column = at % column_bricks
        y0 = jnp.where(valid, (at // column_bricks) * BY, NY)
        lanes = pl.ds(pl.multiple_of((column // tiles) * LANES, LANES), LANES)
        value = pltpu.roll(bricks_ref[s * SUB : (s + 1) * SUB, :], (column % tiles) * BX, 1)
        mask = group == column % tiles
        for g in range(tiles):
            moved = value if g == 0 else pltpu.roll(value, LANES - g * BX, 1)
            rows = pl.ds(pl.multiple_of(y0 + g * SUB, SUB), SUB)
            pltpu.store(plane_ref.at[rows, lanes], moved, mask=mask)
    half = NY // 2
    rows_all = wy_high.shape[0] // 2
    upper = plane_ref[:half, :]
    lower = plane_ref[half:NY, :]
    for p in range(2):
        high, low = split(upper + lower if p == 0 else upper - lower)
        rows = slice(p * rows_all, (p + 1) * rows_all)
        value = dot3(wy_high[rows, :], wy_low[rows, :], high, low)
        for part in range(2):
            for t in range(columns // LANES):
                piece = value[part * rows_all // 2 : (part + 1) * rows_all // 2, t * LANES : (t + 1) * LANES]
                out_ref[part, t, pl.ds(p, rows_all // 2, stride=2), :] = piece


def y_kernel(total, ids_ref, bricks_ref, wy_high, wy_low, out_ref, plane_ref):
    along_y(total, ids_ref, bricks_ref, wy_high, wy_low, plane_ref, out_ref)


def make_y(ids, bricks, tables, columns):
    total = ids.shape[0]
    vmem = pl.BlockSpec(memory_space=pltpu.VMEM)
    return pl.pallas_call(
        functools.partial(y_kernel, total),
        in_specs=[pl.BlockSpec(memory_space=pltpu.SMEM), vmem, vmem, vmem],
        out_specs=vmem,
        out_shape=jax.ShapeDtypeStruct((2, columns // LANES, tables[0].shape[0] // 2, LANES), f32),
        scratch_shapes=[pltpu.VMEM((NY + BY, columns), f32)],
        cost_estimate=pl.CostEstimate(flops=2 * 10**9, bytes_accessed=2 * 10**6, transcendentals=0),
        name="along_y",
    )(ids, bricks, tables[0], tables[1])


def x_kernel(total, half_size, *refs):
    late_refs, refs = refs[: 2 * half_size], refs[2 * half_size :]
    wy_high, wy_low, wx_high, wx_low = refs[:4]
    early_refs, out_ref, plane_ref = refs[4 : 4 + half_size], refs[4 + half_size], refs[5 + half_size]
    late_y_refs = refs[6 + half_size :]
    narrow_size = 2 * half_size
    narrow = lax.axis_index("narrow")
    tiles = early_refs[0].shape[1]
    columns = tiles * LANES
    for k in range(half_size):
        along_y(total, late_refs[2 * k], late_refs[2 * k + 1], wy_high, wy_low, plane_ref, late_y_refs[k])

    def whole(ref, part):
        return jnp.concatenate([ref[part, t] for t in range(tiles)], axis=1)

    u = v = None
    for mask in range(half_size):
        near_ref = early_refs[mask]
        far_ref = late_y_refs[half_size - 1 - mask]
        source = lax.bitwise_xor(narrow, mask)
        mirror = narrow_size - 1 - source
        sign = jnp.where(source < mirror, 1.0, -1.0).astype(f32)
        start = pl.multiple_of((jnp.maximum(source, mirror) - half_size) * columns, columns)
        cos_rows = pl.ds(start, columns)
        sin_rows = pl.ds(pl.multiple_of(NX // 2 + start, columns), columns)
        c = (wx_high[cos_rows, :], wx_low[cos_rows, :])
        s = (wx_high[sin_rows, :], wx_low[sin_rows, :])
        near = [whole(near_ref, part) for part in range(2)]
        far = [whole(far_ref, part) for part in range(2)]
        even = [split(a + b) for a, b in zip(near, far)]
        odd = [split((b - a) * sign) for a, b in zip(near, far)]
        u_new = dot3(*even[0], *c) + dot3(*odd[1], *s)
        v_new = dot3(*even[1], *c) - dot3(*odd[0], *s)
        u = u_new if u is None else u + u_new
        v = v_new if v is None else v + v_new
    lane = lax.broadcasted_iota(i32, (SUB, NX // 2), 1)
    phase_cos, phase_sin = cos_sin_turn((lane * (NX - 1)) % (2 * NX), 2 * NX)
    scale = 1.0 / math.sqrt(NX * NY)
    phase_cos, phase_sin = phase_cos[0:1] * scale, phase_sin[0:1] * scale
    out_ref[0] = u * phase_cos + v * phase_sin
    out_ref[1] = v * phase_cos - u * phase_sin


def make_x(late, tables, early):
    half_size = len(early)
    total = late[0][0].shape[0]
    rows_all = tables[0].shape[0] // 2
    columns = early[0].shape[1] * LANES
    vmem = pl.BlockSpec(memory_space=pltpu.VMEM)
    smem = pl.BlockSpec(memory_space=pltpu.SMEM)
    return pl.pallas_call(
        functools.partial(x_kernel, total, half_size),
        in_specs=[smem, vmem] * half_size + [vmem] * (4 + half_size),
        out_specs=vmem,
        out_shape=jax.ShapeDtypeStruct((2, rows_all, NX // 2), f32),
        scratch_shapes=[pltpu.VMEM((NY + BY, columns), f32)] + [pltpu.VMEM(early[0].shape, f32)] * half_size,
        name="along_x",
    )(*[part for pair in late for part in pair], *tables, *early)


def local(density_blocks, block_groups, block_brick, orbital_freq, orbital_phase, core_density):
    wide_size = lax.axis_size("wide")
    narrow_size = lax.axis_size("narrow")
    block_count = density_blocks.shape[0]
    slots = (2 * block_count + wide_size - 1) // wide_size
    planes, grid_rows, columns = core_density.shape
    half_size = narrow_size // 2
    assert narrow_size & (narrow_size - 1) == 0 and planes == 1 and slots <= SUB
    send = make_pieces(
        density_blocks, block_groups, block_brick, orbital_freq, orbital_phase, wide_size, slots, planes
    )
    got = lax.all_to_all(send, "wide", split_axis=0, concat_axis=0, tiled=True)
    total = wide_size * slots
    ids = got[:, slots * SUB : slots * SUB + slots, 0].astype(i32).reshape(total)
    own = make_energy(got, ids, core_density.reshape(grid_rows, columns), slots)

    def across(value, mask):
        return lax.ppermute(value, "narrow", [(i, i ^ mask) for i in range(narrow_size)])

    def ids_of(bricks):
        return bricks[total * SUB :].reshape(-1)[:total].astype(i32)

    bricks = {0: own}
    step = half_size
    while step:
        bricks |= {mask | step: across(value, step) for mask, value in bricks.items()}
        step //= 2
    tables = make_tables(narrow_size)
    early = [make_y(ids_of(bricks[mask]), bricks[mask], tables, columns) for mask in range(half_size)]
    late = [(ids_of(bricks[mask]), bricks[mask]) for mask in range(half_size, narrow_size)]
    return make_x(late, tables, early)[None]


def solution(mesh):
    return jax.shard_map(
        local,
        mesh=mesh,
        in_specs=(
            P(("wide", "narrow"), None, None),
            P(("wide", "narrow"), None),
            P(("wide", "narrow")),
            P(),
            P(),
            P("wide", None, "narrow"),
        ),
        out_specs=P("wide", None, "narrow", None),
        check_vma=False,
    )
```

```python
import functools
import math

import jax
import jax.numpy as jnp
from jax import lax
from jax.experimental import pallas as pl
from jax.experimental.pallas import tpu as pltpu
from jax.sharding import PartitionSpec as P

NX = 1024
NY = 1024
GRP = 128
BY = 32
BX = 32
LANES = 128
PARTS = 4
SUB = 8

f32 = jnp.float32
bf16 = jnp.bfloat16
i32 = jnp.int32

energy_coef = -0.75 * (3.0 / math.pi) ** (1.0 / 3.0)

COS_FIT = (0.999999989, -0.499999891, 0.0416664892, -0.00138878036, 2.47698836e-05, -2.70790308e-07, 1.72450917e-09)
SIN_FIT = (0.999999999, -0.166666659, 0.00833332129, -0.000198405341, 2.753585e-06, -2.47288117e-08, 1.36130988e-10)
TURN_HI = 6.28125
TURN_LO = 2.0 * math.pi - TURN_HI


def horner(w, fit):
    total = jnp.full_like(w, fit[-1])
    for term in fit[-2::-1]:
        total = total * w + term
    return total


def cos_any(angle):
    turns = jnp.floor(angle * (0.5 / math.pi) + 0.5)
    r = (angle - turns * TURN_HI) - turns * TURN_LO
    return horner(r * r, COS_FIT)


def cos_sin_turn(step, length):
    r = (step - length // 2).astype(f32) * (2.0 * math.pi / length)
    w = r * r
    return -horner(w, COS_FIT), -(r * horner(w, SIN_FIT))


def split(value):
    high = value.astype(bf16)
    return high, (value - high.astype(f32)).astype(bf16)


def dot3(lhs_high, lhs_low, rhs_high, rhs_low):
    dot = functools.partial(jnp.dot, preferred_element_type=f32)
    return dot(lhs_high, rhs_high) + dot(lhs_low, rhs_high) + dot(lhs_high, rhs_low)


def coarse_fine(value):
    shift = 1.5 * 2.0**19
    coarse = (value + shift) - shift
    return coarse, value - coarse


def pieces_kernel(
    count, slots, planes, groups_ref, brick_ref, blocks_ref, freq_ref, phase_ref,
    send_ref, count_ref, stage_ref, sems, mixed0, mixed1, rows0, rows1,
):
    row_bricks = NX // BX
    col_bricks = NY // BY
    wide_size = send_ref.shape[0]
    narrow_size = lax.axis_size("narrow")
    narrow = lax.axis_index("narrow")
    column_bricks = row_bricks // narrow_size
    flip = 2 * narrow < narrow_size
    lane = lax.broadcasted_iota(i32, (SUB, LANES), 1)
    row = lax.broadcasted_iota(i32, (BY, GRP), 0)
    mixed, rows = (mixed0, mixed1), (rows0, rows1)

    def fetch(b):
        return pltpu.make_async_copy(blocks_ref.at[b], stage_ref.at[b], sems.at[b])

    for b in range(count):
        fetch(b).start()
    zero = jnp.zeros((slots * SUB, LANES), f32)
    none = jnp.full((SUB, LANES), -1.0, f32)
    for w in range(wide_size):
        send_ref[w, : slots * SUB, :] = zero
        send_ref[w, slots * SUB :, :] = none
        count_ref[w] = 0

    def factors(side, b):
        q = brick_ref[b]
        xb = q % row_bricks
        yb = (q // row_bricks) % col_bricks
        zb = q // (row_bricks * col_bricks)
        ys = (yb * BY + row).astype(f32)
        xs = (xb * BX + jnp.where(flip, BX - 1 - row, row)).astype(f32)
        at = pl.ds(pl.multiple_of(groups_ref[side, b] * GRP, GRP), GRP)
        freq = freq_ref[:, at]
        phase = phase_ref[:, at]
        along_x = cos_any(xs * freq[0:1] + phase[0:1])
        along_y = cos_any(ys * freq[1:2] + phase[1:2])
        along_z = cos_any(jnp.broadcast_to(zb.astype(f32) * freq[2:3] + phase[2:3], (SUB, GRP)))
        return along_x, along_y * along_z[0:1]

    pair = 2 * SUB

    def prepare(b, k):
        along_x, along_y = factors(0, b)
        xa, xb = coarse_fine(along_x)
        ya, yb = coarse_fine(along_y)
        rows_ref = rows[k]
        rows_ref[0] = xa
        rows_ref[1] = xb
        halves = []
        for h in range(BY // pair):
            at = slice(h * pair, (h + 1) * pair)
            halves.append((ya[at].astype(bf16), yb[at].astype(bf16), along_y[at].astype(bf16)))
        block = jnp.concatenate(split(stage_ref[b]), axis=1)
        block = jnp.concatenate([block, block], axis=0)
        per_part = BY * BX // pair // PARTS
        for part in range(PARTS):
            coarse, fine = [], []
            for tile in range(part * per_part, (part + 1) * per_part):
                x = tile % BX
                y_a, y_b, y_all = halves[tile // BX]
                x_a, x_b = (
                    jnp.concatenate([rows_ref[p, pl.ds(x, SUB, stride=0), :]] * 2, axis=0).astype(bf16)
                    for p in range(2)
                )
                coarse.append(x_a * y_a)
                fine.append(x_a * y_b + x_b * y_all)
            left = jnp.concatenate([jnp.concatenate(coarse, axis=0), jnp.concatenate(fine, axis=0)], axis=1)
            at = slice(part * per_part * pair, (part + 1) * per_part * pair)
            mixed[k][at, :] = jnp.dot(left, block, preferred_element_type=f32)
            yield

    def finish(b, k):
        along_x, along_y = factors(1, b)
        rows_ref = rows[k]
        rows_ref[2] = along_x
        tiles = [along_y[g * SUB : (g + 1) * SUB] for g in range(BY // SUB)]

        def row_sums(first, size):
            if size == 1:
                g, x = first // BX, first % BX
                at = slice((((g // 2) * BX + x) * 2 + g % 2) * SUB, (((g // 2) * BX + x) * 2 + g % 2 + 1) * SUB)
                value = mixed[k][at, :GRP] + mixed[k][at, GRP:]
                return value * (rows_ref[2, pl.ds(x, SUB, stride=0), :] * tiles[g])
            bit = size // 2
            one, two = row_sums(first, bit), row_sums(first + bit, bit)
            return merge(one, two, bit)

        def merge(one, two, bit):
            odd = (lane & bit) != 0
            return jnp.where(odd, two, one) + pltpu.roll(jnp.where(odd, one, two), bit, 1)

        sums = []
        for part in range(PARTS):
            sums.append(row_sums(part * (LANES // PARTS), LANES // PARTS))
            yield
        while len(sums) > 1:
            bit = LANES // len(sums)
            sums = [merge(one, two, bit) for one, two in zip(sums[::2], sums[1::2])]
        value = sums[0]
        q = brick_ref[b]
        zb = q // (row_bricks * col_bricks)
        home = zb // planes
        yb = (q // row_bricks) % col_bricks
        brick = ((zb % planes) * col_bricks + yb) * column_bricks + (q % row_bricks - narrow * column_bricks)
        rank = count_ref[home]
        count_ref[home] = rank + 1
        send_ref[home, pl.ds(pl.multiple_of(rank * SUB, SUB), SUB), :] = value
        send_ref[home, pl.ds(slots * SUB + rank, 1), :] = jnp.full((1, LANES), 1.0, f32) * brick.astype(f32)

    def weave(*works):
        works = list(works)
        while works:
            works = [work for work in works if next(work, works) is not works]

    fetch(0).wait()
    weave(prepare(0, 0))

    def two_blocks(i, carry):
        b = 2 * i
        fetch(b + 1).wait()
        fetch(b + 2).wait()
        weave(prepare(b + 1, 1), finish(b, 0))
        weave(prepare(b + 2, 0), finish(b + 1, 1))
        return carry

    lax.fori_loop(0, count // 2 - 1, two_blocks, 0)
    fetch(count - 1).wait()
    weave(prepare(count - 1, 1), finish(count - 2, 0))
    weave(finish(count - 1, 1))


def make_pieces(blocks, groups, bricks, freq, phase, wide_size, slots, planes):
    count = blocks.shape[0]
    assert count % 2 == 0 and count >= 2
    rows = slots * SUB + SUB
    vmem = pl.BlockSpec(memory_space=pltpu.VMEM)
    smem = pl.BlockSpec(memory_space=pltpu.SMEM)
    mixed = pltpu.VMEM((BY * BX, 2 * GRP), f32)
    return pl.pallas_call(
        functools.partial(pieces_kernel, count, slots, planes),
        in_specs=[smem, smem, pl.BlockSpec(memory_space=pl.ANY), vmem, vmem],
        out_specs=vmem,
        out_shape=jax.ShapeDtypeStruct((wide_size, rows, LANES), f32),
        scratch_shapes=[
            pltpu.SMEM((wide_size,), i32),
            pltpu.VMEM((count, GRP, GRP), f32),
            pltpu.SemaphoreType.DMA((count,)),
            mixed, mixed,
            pltpu.VMEM((3, BX, GRP), f32), pltpu.VMEM((3, BX, GRP), f32),
        ],
        name="pieces",
    )(groups.T, bricks, blocks, freq, phase)


def energy_kernel(slots, got_ref, core_ref, out_ref, ids_ref, first_ref, valence_ref, cells_ref, sem):
    wide_size = got_ref.shape[0]
    total = wide_size * slots
    narrow_size = lax.axis_size("narrow")
    narrow = lax.axis_index("narrow")
    column_bricks = core_ref.shape[1] // BX
    tiles = LANES // BX
    flip = 2 * narrow < narrow_size
    lane = lax.broadcasted_iota(i32, (SUB, LANES), 1)
    sub = lax.broadcasted_iota(i32, (SUB, LANES), 0)
    group = lane // BX

    fetch = pltpu.make_async_copy(got_ref.at[:, pl.ds(slots * SUB, SUB), :], ids_ref, sem)
    fetch.start()

    def piece(s):
        return got_ref[s // slots, (s % slots) * SUB : (s % slots + 1) * SUB, :]

    for s in range(total):
        valence_ref[s * SUB : (s + 1) * SUB, :] = jnp.zeros((SUB, LANES), f32)
    fetch.wait()
    bricks = [jnp.maximum(ids_ref[s // slots, s % slots, 0], 0.0).astype(i32) for s in range(total)]
    for s in range(total - 1, -1, -1):
        first_ref[bricks[s]] = s
    owners = [first_ref[bricks[s]] for s in range(total)]
    for s in range(total):
        rows = pl.ds(pl.multiple_of(owners[s] * SUB, SUB), SUB)
        valence_ref[rows, :] = valence_ref[rows, :] + piece(s)
    head = jnp.full((SUB, LANES), -1.0, f32)
    mirror = jnp.where(flip, lane - lane % BX + (BX - 1 - lane % BX), lane)
    for s in range(total):
        at = bricks[s]
        column = at % column_bricks
        placed = jnp.where(flip, at - column + (column_bricks - 1 - column), at)
        mark = jnp.where(owners[s] == s, placed, -1).astype(f32)
        head = jnp.where((lane == s % LANES) & (sub == s // LANES), mark, head)
        y0 = pl.multiple_of((at // column_bricks) * BY, BY)
        lanes = pl.ds(pl.multiple_of((column // tiles) * LANES, LANES), LANES)
        block = core_ref[pl.ds(y0, BY), lanes]
        first = column % tiles
        value = None
        for g in range(tiles):
            moved = pltpu.roll(block[g * SUB : (g + 1) * SUB], ((g - first + tiles) % tiles) * BX, 1)
            value = moved if value is None else jnp.where(group == g, moved, value)
        cells_ref[s * SUB : (s + 1) * SUB, :] = jnp.take_along_axis(value, mirror, axis=1)

    def four_thirds(value):
        size = jnp.maximum(jnp.abs(value), 1e-30)
        inverse = jnp.exp2(jnp.log2(size) * (-1.0 / 3.0))
        inverse = inverse * (4.0 - size * (inverse * inverse * inverse)) * (1.0 / 3.0)
        return size * (size * (inverse * inverse))

    core = cells_ref[...]
    rho = core + valence_ref[...]
    out_ref[: total * SUB, :] = energy_coef * (four_thirds(rho) - four_thirds(core))
    out_ref[total * SUB :, :] = head


def make_energy(got, core, slots):
    wide_size = got.shape[0]
    total = wide_size * slots
    bricks = (core.shape[0] // BY) * (core.shape[1] // BX)
    vmem = pl.BlockSpec(memory_space=pltpu.VMEM)
    return pl.pallas_call(
        functools.partial(energy_kernel, slots),
        in_specs=[vmem, vmem],
        out_specs=vmem,
        out_shape=jax.ShapeDtypeStruct(((total + 1) * SUB, LANES), f32),
        scratch_shapes=[
            pltpu.SMEM((wide_size, SUB, LANES), f32),
            pltpu.SMEM((bricks,), i32),
            pltpu.VMEM((total * SUB, LANES), f32),
            pltpu.VMEM((total * SUB, LANES), f32),
            pltpu.SemaphoreType.DMA,
        ],
        name="energy",
    )(got, core)


def tables_kernel(wy_high, wy_low, wx_high, wx_low):
    rows_all = NY // lax.axis_size("narrow")
    narrow = lax.axis_index("narrow")
    half = rows_all // 2
    depth = NY // 2
    lane = lax.broadcasted_iota(i32, (half, LANES), 1)
    row = lax.broadcasted_iota(i32, (half, LANES), 0)
    for p in range(2):
        wave = rows_all * narrow + 2 * row + p
        base_cos, base_sin = cos_sin_turn((wave * lane) % NY, NY)
        for t in range(depth // LANES):
            jump_cos, jump_sin = cos_sin_turn((wave[:SUB] * (t * LANES)) % NY, NY)
            jump_cos = jnp.concatenate([jump_cos] * (half // SUB), axis=0)
            jump_sin = jnp.concatenate([jump_sin] * (half // SUB), axis=0)
            at = slice(t * LANES, (t + 1) * LANES)
            for part, value in (
                (0, base_cos * jump_cos - base_sin * jump_sin),
                (1, -(base_sin * jump_cos + base_cos * jump_sin)),
            ):
                rows = slice(p * rows_all + part * half, p * rows_all + (part + 1) * half)
                wy_high[rows, at], wy_low[rows, at] = split(value)
    depth = NX // 2
    lane = lax.broadcasted_iota(i32, (depth, LANES), 1)
    place = 2 * lax.broadcasted_iota(i32, (depth, LANES), 0) + 1
    base_cos, base_sin = cos_sin_turn((place * lane) % (2 * NX), 2 * NX)
    for t in range(NX // 2 // LANES):
        jump_cos, jump_sin = cos_sin_turn((place[:SUB] * (t * LANES)) % (2 * NX), 2 * NX)
        jump_cos = jnp.concatenate([jump_cos] * (depth // SUB), axis=0)
        jump_sin = jnp.concatenate([jump_sin] * (depth // SUB), axis=0)
        at = slice(t * LANES, (t + 1) * LANES)
        for part, value in (
            (0, base_cos * jump_cos - base_sin * jump_sin),
            (1, base_sin * jump_cos + base_cos * jump_sin),
        ):
            rows = slice(part * depth, (part + 1) * depth)
            wx_high[rows, at], wx_low[rows, at] = split(value)


def make_tables(narrow_size):
    rows_all = NY // narrow_size
    y_shape = jax.ShapeDtypeStruct((2 * rows_all, NY // 2), bf16)
    x_shape = jax.ShapeDtypeStruct((NX, NX // 2), bf16)
    vmem = pl.BlockSpec(memory_space=pltpu.VMEM)
    return pl.pallas_call(
        tables_kernel,
        out_specs=[vmem] * 4,
        out_shape=[y_shape, y_shape, x_shape, x_shape],
        name="tables",
    )()


def along_y(total, bricks_ref, wy_high, wy_low, plane_ref, ids_ref, sem, out_ref):
    columns = plane_ref.shape[1]
    column_bricks = columns // BX
    tiles = LANES // BX
    lane = lax.broadcasted_iota(i32, (SUB, LANES), 1)
    group = lane // BX
    fetch = pltpu.make_async_copy(bricks_ref.at[pl.ds(total * SUB, SUB), :], ids_ref, sem)
    fetch.start()
    plane_ref[...] = jnp.zeros(plane_ref.shape, f32)
    fetch.wait()
    for s in range(total):
        brick = ids_ref[s // LANES, s % LANES].astype(i32)
        valid = brick >= 0
        at = jnp.maximum(brick, 0)
        column = at % column_bricks
        y0 = jnp.where(valid, (at // column_bricks) * BY, NY)
        lanes = pl.ds(pl.multiple_of((column // tiles) * LANES, LANES), LANES)
        value = pltpu.roll(bricks_ref[s * SUB : (s + 1) * SUB, :], (column % tiles) * BX, 1)
        mask = group == column % tiles
        for g in range(tiles):
            moved = value if g == 0 else pltpu.roll(value, LANES - g * BX, 1)
            rows = pl.ds(pl.multiple_of(y0 + g * SUB, SUB), SUB)
            pltpu.store(plane_ref.at[rows, lanes], moved, mask=mask)
    half = NY // 2
    rows_all = wy_high.shape[0] // 2
    upper = plane_ref[:half, :]
    lower = plane_ref[half:NY, :]
    for p in range(2):
        high, low = split(upper + lower if p == 0 else upper - lower)
        rows = slice(p * rows_all, (p + 1) * rows_all)
        value = dot3(wy_high[rows, :], wy_low[rows, :], high, low)
        for part in range(2):
            for t in range(columns // LANES):
                piece = value[part * rows_all // 2 : (part + 1) * rows_all // 2, t * LANES : (t + 1) * LANES]
                out_ref[part, t, pl.ds(p, rows_all // 2, stride=2), :] = piece


def y_kernel(total, bricks_ref, wy_high, wy_low, out_ref, plane_ref, ids_ref, sem):
    along_y(total, bricks_ref, wy_high, wy_low, plane_ref, ids_ref, sem, out_ref)


def make_y(bricks, tables, columns):
    total = bricks.shape[0] // SUB - 1
    vmem = pl.BlockSpec(memory_space=pltpu.VMEM)
    return pl.pallas_call(
        functools.partial(y_kernel, total),
        in_specs=[vmem, vmem, vmem],
        out_specs=vmem,
        out_shape=jax.ShapeDtypeStruct((2, columns // LANES, tables[0].shape[0] // 2, LANES), f32),
        scratch_shapes=[pltpu.VMEM((NY + BY, columns), f32), pltpu.SMEM((SUB, LANES), f32), pltpu.SemaphoreType.DMA],
        cost_estimate=pl.CostEstimate(flops=2 * 10**9, bytes_accessed=2 * 10**6, transcendentals=0),
        name="along_y",
    )(bricks, tables[0], tables[1])


def x_kernel(total, half_size, *refs):
    late_refs, refs = refs[:half_size], refs[half_size:]
    wy_high, wy_low, wx_high, wx_low = refs[:4]
    early_refs, out_ref, plane_ref = refs[4 : 4 + half_size], refs[4 + half_size], refs[5 + half_size]
    ids_ref, sem = refs[6 + half_size : 8 + half_size]
    late_y_refs = refs[8 + half_size :]
    narrow_size = 2 * half_size
    narrow = lax.axis_index("narrow")
    tiles = early_refs[0].shape[1]
    columns = tiles * LANES
    for k in range(half_size):
        along_y(total, late_refs[k], wy_high, wy_low, plane_ref, ids_ref, sem, late_y_refs[k])

    def whole(ref, part):
        return jnp.concatenate([ref[part, t] for t in range(tiles)], axis=1)

    u = v = None
    for mask in range(half_size):
        near_ref = early_refs[mask]
        far_ref = late_y_refs[half_size - 1 - mask]
        source = lax.bitwise_xor(narrow, mask)
        mirror = narrow_size - 1 - source
        sign = jnp.where(source < mirror, 1.0, -1.0).astype(f32)
        start = pl.multiple_of((jnp.maximum(source, mirror) - half_size) * columns, columns)
        cos_rows = pl.ds(start, columns)
        sin_rows = pl.ds(pl.multiple_of(NX // 2 + start, columns), columns)
        c = (wx_high[cos_rows, :], wx_low[cos_rows, :])
        s = (wx_high[sin_rows, :], wx_low[sin_rows, :])
        near = [whole(near_ref, part) for part in range(2)]
        far = [whole(far_ref, part) for part in range(2)]
        even = [split(a + b) for a, b in zip(near, far)]
        odd = [split((b - a) * sign) for a, b in zip(near, far)]
        u_new = dot3(*even[0], *c) + dot3(*odd[1], *s)
        v_new = dot3(*even[1], *c) - dot3(*odd[0], *s)
        u = u_new if u is None else u + u_new
        v = v_new if v is None else v + v_new
    lane = lax.broadcasted_iota(i32, (SUB, NX // 2), 1)
    phase_cos, phase_sin = cos_sin_turn((lane * (NX - 1)) % (2 * NX), 2 * NX)
    scale = 1.0 / math.sqrt(NX * NY)
    phase_cos, phase_sin = phase_cos[0:1] * scale, phase_sin[0:1] * scale
    out_ref[0] = u * phase_cos + v * phase_sin
    out_ref[1] = v * phase_cos - u * phase_sin


def make_x(late, tables, early):
    half_size = len(early)
    total = late[0].shape[0] // SUB - 1
    rows_all = tables[0].shape[0] // 2
    columns = early[0].shape[1] * LANES
    vmem = pl.BlockSpec(memory_space=pltpu.VMEM)
    return pl.pallas_call(
        functools.partial(x_kernel, total, half_size),
        in_specs=[vmem] * (4 + 2 * half_size),
        out_specs=vmem,
        out_shape=jax.ShapeDtypeStruct((2, rows_all, NX // 2), f32),
        scratch_shapes=[pltpu.VMEM((NY + BY, columns), f32), pltpu.SMEM((SUB, LANES), f32), pltpu.SemaphoreType.DMA]
        + [pltpu.VMEM(early[0].shape, f32)] * half_size,
        name="along_x",
    )(*late, *tables, *early)


def local(density_blocks, block_groups, block_brick, orbital_freq, orbital_phase, core_density):
    wide_size = lax.axis_size("wide")
    narrow_size = lax.axis_size("narrow")
    block_count = density_blocks.shape[0]
    slots = (2 * block_count + wide_size - 1) // wide_size
    planes, grid_rows, columns = core_density.shape
    half_size = narrow_size // 2
    assert narrow_size & (narrow_size - 1) == 0 and planes == 1 and slots <= SUB
    send = make_pieces(
        density_blocks, block_groups, block_brick, orbital_freq, orbital_phase, wide_size, slots, planes
    )
    got = lax.all_to_all(send, "wide", split_axis=0, concat_axis=0, tiled=True)
    own = make_energy(got, core_density.reshape(grid_rows, columns), slots)

    def across(value, mask):
        return lax.ppermute(value, "narrow", [(i, i ^ mask) for i in range(narrow_size)])

    bricks = {0: own}
    step = half_size
    while step:
        bricks |= {mask | step: across(value, step) for mask, value in bricks.items()}
        step //= 2
    tables = make_tables(narrow_size)
    early = [make_y(bricks[mask], tables, columns) for mask in range(half_size)]
    late = [bricks[mask] for mask in range(half_size, narrow_size)]
    return make_x(late, tables, early)[None]


def solution(mesh):
    return jax.shard_map(
        local,
        mesh=mesh,
        in_specs=(
            P(("wide", "narrow"), None, None),
            P(("wide", "narrow"), None),
            P(("wide", "narrow")),
            P(),
            P(),
            P("wide", None, "narrow"),
        ),
        out_specs=P("wide", None, "narrow", None),
        check_vma=False,
    )
```

```python
import functools
import math

import jax
import jax.numpy as jnp
from jax import lax
from jax.experimental import pallas as pl
from jax.experimental.pallas import tpu as pltpu
from jax.sharding import PartitionSpec as P

NX = 1024
NY = 1024
GRP = 128
BY = 32
BX = 32
LANES = 128
PARTS = 4
VMEM_LIMIT = 16 * 2**20
SUB = 8

f32 = jnp.float32
bf16 = jnp.bfloat16
i32 = jnp.int32

energy_coef = -0.75 * (3.0 / math.pi) ** (1.0 / 3.0)

COS_FIT = (0.999999989, -0.499999891, 0.0416664892, -0.00138878036, 2.47698836e-05, -2.70790308e-07, 1.72450917e-09)
SIN_FIT = (0.999999999, -0.166666659, 0.00833332129, -0.000198405341, 2.753585e-06, -2.47288117e-08, 1.36130988e-10)
TURN_HI = 6.28125
TURN_LO = 2.0 * math.pi - TURN_HI


def horner(w, fit):
    total = jnp.full_like(w, fit[-1])
    for term in fit[-2::-1]:
        total = total * w + term
    return total


def cos_any(angle):
    turns = jnp.floor(angle * (0.5 / math.pi) + 0.5)
    r = (angle - turns * TURN_HI) - turns * TURN_LO
    return horner(r * r, COS_FIT)


def cos_sin_turn(step, length):
    r = (step - length // 2).astype(f32) * (2.0 * math.pi / length)
    w = r * r
    return -horner(w, COS_FIT), -(r * horner(w, SIN_FIT))


def on_chip(value):
    return pltpu.with_memory_space_constraint(value, pltpu.VMEM)


def off_chip(value):
    return pltpu.with_memory_space_constraint(value, pltpu.HBM)


def split(value):
    high = value.astype(bf16)
    return high, (value - high.astype(f32)).astype(bf16)


def dot3(lhs_high, lhs_low, rhs_high, rhs_low):
    dot = functools.partial(jnp.dot, preferred_element_type=f32)
    return dot(lhs_high, rhs_high) + dot(lhs_low, rhs_high) + dot(lhs_high, rhs_low)


def coarse_fine(value):
    shift = 1.5 * 2.0**19
    coarse = (value + shift) - shift
    return coarse, value - coarse


def pieces_kernel(
    count, slots, planes, groups_ref, brick_ref, blocks_ref, freq_ref, phase_ref,
    send_ref, count_ref, stage_ref, sems, mixed0, mixed1, rows0, rows1,
):
    row_bricks = NX // BX
    col_bricks = NY // BY
    wide_size = send_ref.shape[0]
    narrow_size = lax.axis_size("narrow")
    narrow = lax.axis_index("narrow")
    column_bricks = row_bricks // narrow_size
    flip = 2 * narrow < narrow_size
    lane = lax.broadcasted_iota(i32, (SUB, LANES), 1)
    row = lax.broadcasted_iota(i32, (BY, GRP), 0)
    mixed, rows = (mixed0, mixed1), (rows0, rows1)

    def fetch(b):
        return pltpu.make_async_copy(blocks_ref.at[b], stage_ref.at[b], sems.at[b])

    for b in range(count):
        fetch(b).start()
    zero = jnp.zeros((slots * SUB, LANES), f32)
    none = jnp.full((SUB, LANES), -1.0, f32)
    for w in range(wide_size):
        send_ref[w, : slots * SUB, :] = zero
        send_ref[w, slots * SUB :, :] = none
        count_ref[w] = 0

    def factors(side, b):
        q = brick_ref[b]
        xb = q % row_bricks
        yb = (q // row_bricks) % col_bricks
        zb = q // (row_bricks * col_bricks)
        ys = (yb * BY + row).astype(f32)
        xs = (xb * BX + jnp.where(flip, BX - 1 - row, row)).astype(f32)
        at = pl.ds(pl.multiple_of(groups_ref[side, b] * GRP, GRP), GRP)
        freq = freq_ref[:, at]
        phase = phase_ref[:, at]
        along_x = cos_any(xs * freq[0:1] + phase[0:1])
        along_y = cos_any(ys * freq[1:2] + phase[1:2])
        along_z = cos_any(jnp.broadcast_to(zb.astype(f32) * freq[2:3] + phase[2:3], (SUB, GRP)))
        return along_x, along_y * along_z[0:1]

    pair = 2 * SUB

    def prepare(b, k):
        along_x, along_y = factors(0, b)
        xa, xb = coarse_fine(along_x)
        ya, yb = coarse_fine(along_y)
        rows_ref = rows[k]
        rows_ref[0] = xa
        rows_ref[1] = xb
        halves = []
        for h in range(BY // pair):
            at = slice(h * pair, (h + 1) * pair)
            halves.append((ya[at].astype(bf16), yb[at].astype(bf16), along_y[at].astype(bf16)))
        block = jnp.concatenate(split(stage_ref[b]), axis=1)
        block = jnp.concatenate([block, block], axis=0)
        per_part = BY * BX // pair // PARTS
        for part in range(PARTS):
            coarse, fine = [], []
            for tile in range(part * per_part, (part + 1) * per_part):
                x = tile % BX
                y_a, y_b, y_all = halves[tile // BX]
                x_a, x_b = (
                    jnp.concatenate([rows_ref[p, pl.ds(x, SUB, stride=0), :]] * 2, axis=0).astype(bf16)
                    for p in range(2)
                )
                coarse.append(x_a * y_a)
                fine.append(x_a * y_b + x_b * y_all)
            left = jnp.concatenate([jnp.concatenate(coarse, axis=0), jnp.concatenate(fine, axis=0)], axis=1)
            at = slice(part * per_part * pair, (part + 1) * per_part * pair)
            mixed[k][at, :] = jnp.dot(left, block, preferred_element_type=f32)
            yield

    def finish(b, k):
        along_x, along_y = factors(1, b)
        rows_ref = rows[k]
        rows_ref[2] = along_x
        tiles = [along_y[g * SUB : (g + 1) * SUB] for g in range(BY // SUB)]

        def row_sums(first, size):
            if size == 1:
                g, x = first // BX, first % BX
                at = slice((((g // 2) * BX + x) * 2 + g % 2) * SUB, (((g // 2) * BX + x) * 2 + g % 2 + 1) * SUB)
                value = mixed[k][at, :GRP] + mixed[k][at, GRP:]
                return value * (rows_ref[2, pl.ds(x, SUB, stride=0), :] * tiles[g])
            bit = size // 2
            one, two = row_sums(first, bit), row_sums(first + bit, bit)
            return merge(one, two, bit)

        def merge(one, two, bit):
            odd = (lane & bit) != 0
            return jnp.where(odd, two, one) + pltpu.roll(jnp.where(odd, one, two), bit, 1)

        sums = []
        for part in range(PARTS):
            sums.append(row_sums(part * (LANES // PARTS), LANES // PARTS))
            yield
        while len(sums) > 1:
            bit = LANES // len(sums)
            sums = [merge(one, two, bit) for one, two in zip(sums[::2], sums[1::2])]
        value = sums[0]
        q = brick_ref[b]
        zb = q // (row_bricks * col_bricks)
        home = zb // planes
        yb = (q // row_bricks) % col_bricks
        brick = ((zb % planes) * col_bricks + yb) * column_bricks + (q % row_bricks - narrow * column_bricks)
        rank = count_ref[home]
        count_ref[home] = rank + 1
        send_ref[home, pl.ds(pl.multiple_of(rank * SUB, SUB), SUB), :] = value
        head = send_ref[home, slots * SUB :, :]
        send_ref[home, slots * SUB :, :] = jnp.where(lane == rank, brick.astype(f32), head)

    def weave(*works):
        works = list(works)
        while works:
            works = [work for work in works if next(work, works) is not works]

    fetch(0).wait()
    weave(prepare(0, 0))

    def two_blocks(i, carry):
        b = 2 * i
        fetch(b + 1).wait()
        fetch(b + 2).wait()
        weave(prepare(b + 1, 1), finish(b, 0))
        weave(prepare(b + 2, 0), finish(b + 1, 1))
        return carry

    lax.fori_loop(0, count // 2 - 1, two_blocks, 0)
    fetch(count - 1).wait()
    weave(prepare(count - 1, 1), finish(count - 2, 0))
    weave(finish(count - 1, 1))


def make_pieces(blocks, groups, bricks, freq, phase, wide_size, slots, planes):
    count = blocks.shape[0]
    assert count % 2 == 0 and count >= 2
    rows = slots * SUB + SUB
    vmem = pl.BlockSpec(memory_space=pltpu.VMEM)
    smem = pl.BlockSpec(memory_space=pltpu.SMEM)
    mixed = pltpu.VMEM((BY * BX, 2 * GRP), f32)
    return pl.pallas_call(
        functools.partial(pieces_kernel, count, slots, planes),
        in_specs=[smem, smem, pl.BlockSpec(memory_space=pl.ANY), vmem, vmem],
        out_specs=vmem,
        out_shape=pltpu.VMEM((wide_size, rows, LANES), f32),
        scratch_shapes=[
            pltpu.SMEM((wide_size,), i32),
            pltpu.VMEM((count, GRP, GRP), f32),
            pltpu.SemaphoreType.DMA((count,)),
            mixed, mixed,
            pltpu.VMEM((3, BX, GRP), f32), pltpu.VMEM((3, BX, GRP), f32),
        ],
        compiler_params=pltpu.CompilerParams(vmem_limit_bytes=VMEM_LIMIT),
        name="pieces",
    )(*map(off_chip, (groups.T, bricks, blocks, freq, phase)))


def bits_of(count):
    assert count & (count - 1) == 0
    return count.bit_length() - 1


def energy_kernel(slots, got_ref, core_ref, out_ref, codes_ref, code_ref, first_ref, valence_ref, cells_ref, sem):
    wide_size = got_ref.shape[0]
    total = wide_size * slots
    narrow_size = lax.axis_size("narrow")
    narrow = lax.axis_index("narrow")
    column_bricks = core_ref.shape[1] // BX
    column_bits = bits_of(column_bricks)
    tiles = LANES // BX
    flip = 2 * narrow < narrow_size
    lane = lax.broadcasted_iota(i32, (SUB, LANES), 1)
    sub = lax.broadcasted_iota(i32, (SUB, LANES), 0)
    group = lane // BX

    heads = []
    for w in range(0, wide_size, SUB):
        head = jnp.concatenate([got_ref[w + k, slots * SUB : slots * SUB + 1, :] for k in range(SUB)], axis=0)
        heads.append(head)
        codes_ref[w : w + SUB, :] = jnp.maximum(head, 0.0).astype(i32)
    fetch = pltpu.make_async_copy(codes_ref, code_ref, sem)
    fetch.start()

    def piece(s):
        return got_ref[s // slots, (s % slots) * SUB : (s % slots + 1) * SUB, :]

    for s in range(total):
        valence_ref[s * SUB : (s + 1) * SUB, :] = jnp.zeros((SUB, LANES), f32)
    mirror = jnp.where(flip, lane - lane % BX + (BX - 1 - lane % BX), lane)
    fetch.wait()
    bricks = [code_ref[s // slots, s % slots] for s in range(total)]
    for s in range(total - 1, -1, -1):
        first_ref[bricks[s]] = s
    for s in range(total):
        owner = first_ref[bricks[s]]
        rows = pl.ds(pl.multiple_of(owner * SUB, SUB), SUB)
        valence_ref[rows, :] = valence_ref[rows, :] + piece(s)
        mark = jnp.where(owner == s, bricks[s], -1).astype(f32)
        w = s // slots
        heads[w // SUB] = jnp.where((lane == s % slots) & (sub == w % SUB), mark, heads[w // SUB])
        column = bricks[s] & (column_bricks - 1)
        y0 = pl.multiple_of((bricks[s] >> column_bits) * BY, BY)
        lanes = pl.ds(pl.multiple_of((column >> bits_of(tiles)) * LANES, LANES), LANES)
        first = column & (tiles - 1)
        value = None
        for g in range(tiles):
            block = core_ref[pl.ds(y0 + g * SUB, SUB), lanes]
            moved = pltpu.roll(block, ((g - first) & (tiles - 1)) * BX, 1)
            value = moved if value is None else jnp.where(group == g, moved, value)
        cells_ref[s * SUB : (s + 1) * SUB, :] = jnp.take_along_axis(value, mirror, axis=1)

    def four_thirds(value):
        size = jnp.maximum(jnp.abs(value), 1e-30)
        inverse = jnp.exp2(jnp.log2(size) * (-1.0 / 3.0))
        inverse = inverse * (4.0 - size * (inverse * inverse * inverse)) * (1.0 / 3.0)
        return size * (size * (inverse * inverse))

    core = cells_ref[...]
    rho = core + valence_ref[...]
    out_ref[: total * SUB, :] = energy_coef * (four_thirds(rho) - four_thirds(core))
    for k, head in enumerate(heads):
        code = jnp.maximum(head, 0.0).astype(i32)
        column = code & (column_bricks - 1)
        placed = jnp.where(flip, code - column + (column_bricks - 1 - column), code)
        rows = slice(total * SUB + k * SUB, total * SUB + (k + 1) * SUB)
        out_ref[rows, :] = jnp.where(head < 0.0, -1.0, placed.astype(f32))


def make_energy(got, core, slots):
    wide_size = got.shape[0]
    total = wide_size * slots
    bricks = (core.shape[0] // BY) * (core.shape[1] // BX)
    vmem = pl.BlockSpec(memory_space=pltpu.VMEM)
    return pl.pallas_call(
        functools.partial(energy_kernel, slots),
        in_specs=[vmem, vmem],
        out_specs=vmem,
        out_shape=pltpu.VMEM((total * SUB + wide_size, LANES), f32),
        scratch_shapes=[
            pltpu.VMEM((wide_size, LANES), i32),
            pltpu.SMEM((wide_size, LANES), i32),
            pltpu.SMEM((bricks,), i32),
            pltpu.VMEM((total * SUB, LANES), f32),
            pltpu.VMEM((total * SUB, LANES), f32),
            pltpu.SemaphoreType.DMA,
        ],
        compiler_params=pltpu.CompilerParams(vmem_limit_bytes=VMEM_LIMIT),
        name="energy",
    )(on_chip(got), core)


def tables_kernel(wy_high, wy_low, wx_high, wx_low):
    rows_all = NY // lax.axis_size("narrow")
    narrow = lax.axis_index("narrow")
    half = rows_all // 2
    depth = NY // 2
    lane = lax.broadcasted_iota(i32, (half, LANES), 1)
    row = lax.broadcasted_iota(i32, (half, LANES), 0)
    for p in range(2):
        wave = rows_all * narrow + 2 * row + p
        base_cos, base_sin = cos_sin_turn((wave * lane) % NY, NY)
        for t in range(depth // LANES):
            jump_cos, jump_sin = cos_sin_turn((wave[:SUB] * (t * LANES)) % NY, NY)
            jump_cos = jnp.concatenate([jump_cos] * (half // SUB), axis=0)
            jump_sin = jnp.concatenate([jump_sin] * (half // SUB), axis=0)
            at = slice(t * LANES, (t + 1) * LANES)
            for part, value in (
                (0, base_cos * jump_cos - base_sin * jump_sin),
                (1, -(base_sin * jump_cos + base_cos * jump_sin)),
            ):
                rows = slice(p * rows_all + part * half, p * rows_all + (part + 1) * half)
                wy_high[rows, at], wy_low[rows, at] = split(value)
    depth = NX // 2
    lane = lax.broadcasted_iota(i32, (depth, LANES), 1)
    place = 2 * lax.broadcasted_iota(i32, (depth, LANES), 0) + 1
    base_cos, base_sin = cos_sin_turn((place * lane) % (2 * NX), 2 * NX)
    for t in range(NX // 2 // LANES):
        jump_cos, jump_sin = cos_sin_turn((place[:SUB] * (t * LANES)) % (2 * NX), 2 * NX)
        jump_cos = jnp.concatenate([jump_cos] * (depth // SUB), axis=0)
        jump_sin = jnp.concatenate([jump_sin] * (depth // SUB), axis=0)
        at = slice(t * LANES, (t + 1) * LANES)
        for part, value in (
            (0, base_cos * jump_cos - base_sin * jump_sin),
            (1, base_sin * jump_cos + base_cos * jump_sin),
        ):
            rows = slice(part * depth, (part + 1) * depth)
            wx_high[rows, at], wx_low[rows, at] = split(value)


def make_tables(narrow_size):
    rows_all = NY // narrow_size
    y_shape = pltpu.VMEM((2 * rows_all, NY // 2), bf16)
    x_shape = pltpu.VMEM((NX, NX // 2), bf16)
    vmem = pl.BlockSpec(memory_space=pltpu.VMEM)
    return pl.pallas_call(
        tables_kernel,
        out_specs=[vmem] * 4,
        out_shape=[y_shape, y_shape, x_shape, x_shape],
        compiler_params=pltpu.CompilerParams(vmem_limit_bytes=VMEM_LIMIT),
        name="tables",
    )()


def along_y(slots, columns, bricks_ref, wy_high, wy_low, scratch, out_ref):
    plane_ref, codes_ref, code_ref, sem = scratch
    wide_size = codes_ref.shape[0]
    total = wide_size * slots
    column_bits = bits_of(columns // BX)
    tiles = LANES // BX
    blocks = columns // LANES
    depth = NY + BY
    group = lax.broadcasted_iota(i32, (SUB, LANES), 1) // BX
    head = bricks_ref[total * SUB :, :]
    brick = jnp.maximum(head, 0.0).astype(i32)
    column = brick & (columns // BX - 1)
    row = (column >> bits_of(tiles)) * depth + jnp.where(head < 0.0, NY, (brick >> column_bits) * BY)
    codes_ref[...] = row * tiles + (column & (tiles - 1))
    fetch = pltpu.make_async_copy(codes_ref, code_ref, sem)
    fetch.start()
    plane_ref[...] = jnp.zeros(plane_ref.shape, f32)
    fetch.wait()
    for s in range(total):
        code = code_ref[s // slots, s % slots]
        first = code & (tiles - 1)
        row = code >> bits_of(tiles)
        value = pltpu.roll(bricks_ref[s * SUB : (s + 1) * SUB, :], first * BX, 1)
        mask = group == first
        for g in range(tiles):
            moved = value if g == 0 else pltpu.roll(value, LANES - g * BX, 1)
            rows = pl.ds(pl.multiple_of(row + g * SUB, SUB), SUB)
            pltpu.store(plane_ref.at[rows, :], moved, mask=mask)
    half = NY // 2
    rows_all = wy_high.shape[0] // 2
    upper = jnp.concatenate([plane_ref[t * depth : t * depth + half, :] for t in range(blocks)], axis=1)
    lower = jnp.concatenate([plane_ref[t * depth + half : t * depth + NY, :] for t in range(blocks)], axis=1)
    dot = functools.partial(jnp.dot, preferred_element_type=f32)
    for p in range(2):
        high, low = split(upper + lower if p == 0 else upper - lower)
        rows = slice(p * rows_all, (p + 1) * rows_all)
        table = wy_high[rows, :]
        value = dot(jnp.concatenate([table, wy_low[rows, :]], axis=0), high)
        value = value[:rows_all] + value[rows_all:] + dot(table, low)
        for part in range(2):
            for t in range(blocks):
                piece = value[part * rows_all // 2 : (part + 1) * rows_all // 2, t * LANES : (t + 1) * LANES]
                out_ref[part, t, pl.ds(p, rows_all // 2, stride=2), :] = piece


def along_y_scratch(wide_size, columns):
    return [
        pltpu.VMEM((columns // LANES * (NY + BY), LANES), f32),
        pltpu.VMEM((wide_size, LANES), i32),
        pltpu.SMEM((wide_size, LANES), i32),
        pltpu.SemaphoreType.DMA,
    ]


def y_kernel(slots, columns, bricks_ref, wy_high, wy_low, out_ref, *scratch):
    along_y(slots, columns, bricks_ref, wy_high, wy_low, scratch, out_ref)


def make_y(bricks, tables, columns, wide_size, slots):
    vmem = pl.BlockSpec(memory_space=pltpu.VMEM)
    return pl.pallas_call(
        functools.partial(y_kernel, slots, columns),
        in_specs=[vmem, vmem, vmem],
        out_specs=vmem,
        out_shape=pltpu.VMEM((2, columns // LANES, tables[0].shape[0] // 2, LANES), f32),
        scratch_shapes=along_y_scratch(wide_size, columns),
        cost_estimate=pl.CostEstimate(flops=2 * 10**9, bytes_accessed=2 * 10**6, transcendentals=0),
        compiler_params=pltpu.CompilerParams(vmem_limit_bytes=VMEM_LIMIT),
        name="along_y",
    )(on_chip(bricks), on_chip(tables[0]), on_chip(tables[1]))


def x_kernel(slots, columns, mask, first, last, *refs):
    bricks_ref, near_ref, wy_high, wy_low, wx_high, wx_low = refs[:6]
    sum_ref = None if first else refs[6]
    out_ref, far_ref = refs[6 + (not first)], refs[7 + (not first)]
    scratch = refs[8 + (not first) :]
    half_size = lax.axis_size("narrow") // 2
    narrow = lax.axis_index("narrow")
    blocks = columns // LANES
    along_y(slots, columns, bricks_ref, wy_high, wy_low, scratch, far_ref)

    def whole(ref, part):
        return jnp.concatenate([ref[part, t] for t in range(blocks)], axis=1)

    source = lax.bitwise_xor(narrow, mask)
    mirror = 2 * half_size - 1 - source
    sign = jnp.where(source < mirror, 1.0, -1.0).astype(f32)
    start = pl.multiple_of((jnp.maximum(source, mirror) - half_size) * columns, columns)
    cos_rows = pl.ds(start, columns)
    sin_rows = pl.ds(pl.multiple_of(NX // 2 + start, columns), columns)
    near = [whole(near_ref, part) for part in range(2)]
    far = [whole(far_ref, part) for part in range(2)]
    even = jnp.concatenate([a + b for a, b in zip(near, far)], axis=0)
    odd = jnp.concatenate([(far[1] - near[1]) * sign, (near[0] - far[0]) * sign], axis=0)
    even_high, even_low = split(even)
    odd_high, odd_low = split(odd)
    both = jnp.dot(
        jnp.concatenate([even_high, even_low, even_high, odd_high, odd_low, odd_high], axis=1),
        jnp.concatenate(
            [
                wx_high[cos_rows, :], wx_high[cos_rows, :], wx_low[cos_rows, :],
                wx_high[sin_rows, :], wx_high[sin_rows, :], wx_low[sin_rows, :],
            ],
            axis=0,
        ),
        preferred_element_type=f32,
    )
    rows_all = wy_high.shape[0] // 2
    u, v = both[:rows_all], both[rows_all:]
    if not first:
        u, v = u + sum_ref[0], v + sum_ref[1]
    if last:
        lane = lax.broadcasted_iota(i32, (SUB, NX // 2), 1)
        phase_cos, phase_sin = cos_sin_turn((lane * (NX - 1)) % (2 * NX), 2 * NX)
        scale = 1.0 / math.sqrt(NX * NY)
        phase_cos, phase_sin = phase_cos[0:1] * scale, phase_sin[0:1] * scale
        u, v = u * phase_cos + v * phase_sin, v * phase_cos - u * phase_sin
    out_ref[0] = u
    out_ref[1] = v


def make_x(bricks, near, mask, tables, total, last, wide_size, slots):
    first = total is None
    rows_all = tables[0].shape[0] // 2
    columns = near.shape[1] * LANES
    vmem = pl.BlockSpec(memory_space=pltpu.VMEM)
    args = (bricks, near, *tables) if first else (bricks, near, *tables, total)
    return pl.pallas_call(
        functools.partial(x_kernel, slots, columns, mask, first, last),
        in_specs=[vmem] * len(args),
        out_specs=vmem,
        out_shape=(jax.ShapeDtypeStruct if last else pltpu.VMEM)((2, rows_all, NX // 2), f32),
        scratch_shapes=[pltpu.VMEM(near.shape, f32)] + along_y_scratch(wide_size, columns),
        compiler_params=pltpu.CompilerParams(vmem_limit_bytes=VMEM_LIMIT),
        name="along_x",
    )(*map(on_chip, args))


def local(density_blocks, block_groups, block_brick, orbital_freq, orbital_phase, core_density):
    wide_size = lax.axis_size("wide")
    narrow_size = lax.axis_size("narrow")
    block_count = density_blocks.shape[0]
    slots = (2 * block_count + wide_size - 1) // wide_size
    planes, grid_rows, columns = core_density.shape
    half_size = narrow_size // 2
    assert narrow_size & (narrow_size - 1) == 0 and planes == 1 and slots <= LANES
    send = make_pieces(
        density_blocks, block_groups, block_brick, orbital_freq, orbital_phase, wide_size, slots, planes
    )
    got = lax.all_to_all(send, "wide", split_axis=0, concat_axis=0, tiled=True)
    own = make_energy(got, core_density.reshape(grid_rows, columns), slots)

    def across(value, mask):
        return lax.ppermute(value, "narrow", [(i, i ^ mask) for i in range(narrow_size)])

    bricks = {0: own}
    step = half_size
    while step:
        bricks |= {mask | step: across(value, step) for mask, value in bricks.items()}
        step //= 2
    tables = make_tables(narrow_size)
    early = [make_y(bricks[mask], tables, columns, wide_size, slots) for mask in range(half_size)]
    total = None
    for late in range(half_size, narrow_size):
        mask = narrow_size - 1 - late
        total = make_x(
            bricks[late], early[mask], mask, tables, total, late == narrow_size - 1, wide_size, slots
        )
    return total[None]


def solution(mesh):
    return jax.shard_map(
        local,
        mesh=mesh,
        in_specs=(
            P(("wide", "narrow"), None, None),
            P(("wide", "narrow"), None),
            P(("wide", "narrow")),
            P(),
            P(),
            P("wide", None, "narrow"),
        ),
        out_specs=P("wide", None, "narrow", None),
        check_vma=False,
    )
```

```python
import functools
import math

import jax
import jax.numpy as jnp
from jax import lax
from jax.experimental import pallas as pl
from jax.experimental.pallas import tpu as pltpu
from jax.sharding import PartitionSpec as P

NX = 1024
NY = 1024
GRP = 128
BY = 32
BX = 32
LANES = 128
PARTS = 4
VMEM_LIMIT = 16 * 2**20
SUB = 8

f32 = jnp.float32
bf16 = jnp.bfloat16
i32 = jnp.int32

energy_coef = -0.75 * (3.0 / math.pi) ** (1.0 / 3.0)

COS_FIT = (0.999999989, -0.499999891, 0.0416664892, -0.00138878036, 2.47698836e-05, -2.70790308e-07, 1.72450917e-09)
SIN_FIT = (0.999999999, -0.166666659, 0.00833332129, -0.000198405341, 2.753585e-06, -2.47288117e-08, 1.36130988e-10)
TURN_HI = 6.28125
TURN_LO = 2.0 * math.pi - TURN_HI


def horner(w, fit):
    total = jnp.full_like(w, fit[-1])
    for term in fit[-2::-1]:
        total = total * w + term
    return total


def cos_any(angle):
    turns = jnp.floor(angle * (0.5 / math.pi) + 0.5)
    r = (angle - turns * TURN_HI) - turns * TURN_LO
    return horner(r * r, COS_FIT)


def cos_sin_turn(step, length):
    r = (step - length // 2).astype(f32) * (2.0 * math.pi / length)
    w = r * r
    return -horner(w, COS_FIT), -(r * horner(w, SIN_FIT))


def on_chip(value):
    return pltpu.with_memory_space_constraint(value, pltpu.VMEM)


def off_chip(value):
    return pltpu.with_memory_space_constraint(value, pltpu.HBM)


def split(value):
    high = value.astype(bf16)
    return high, (value - high.astype(f32)).astype(bf16)


def dot3(lhs_high, lhs_low, rhs_high, rhs_low):
    dot = functools.partial(jnp.dot, preferred_element_type=f32)
    return dot(lhs_high, rhs_high) + dot(lhs_low, rhs_high) + dot(lhs_high, rhs_low)


def coarse_fine(value):
    shift = 1.5 * 2.0**19
    coarse = (value + shift) - shift
    return coarse, value - coarse


def pieces_kernel(
    count, slots, planes, groups_ref, brick_ref, blocks_ref, freq_ref, phase_ref,
    send_ref, count_ref, stage_ref, sems, mixed0, mixed1, rows0, rows1,
):
    row_bricks = NX // BX
    col_bricks = NY // BY
    wide_size = send_ref.shape[0]
    narrow_size = lax.axis_size("narrow")
    narrow = lax.axis_index("narrow")
    column_bricks = row_bricks // narrow_size
    flip = 2 * narrow < narrow_size
    lane = lax.broadcasted_iota(i32, (SUB, LANES), 1)
    row = lax.broadcasted_iota(i32, (BY, GRP), 0)
    mixed, rows = (mixed0, mixed1), (rows0, rows1)

    def fetch(b):
        return pltpu.make_async_copy(blocks_ref.at[b], stage_ref.at[b], sems.at[b])

    for b in range(count):
        fetch(b).start()
    zero = jnp.zeros((slots * SUB, LANES), f32)
    none = jnp.full((SUB, LANES), -1.0, f32)
    for w in range(wide_size):
        send_ref[w, : slots * SUB, :] = zero
        send_ref[w, slots * SUB :, :] = none
        count_ref[w] = 0

    def factors(side, b):
        q = brick_ref[b]
        xb = q % row_bricks
        yb = (q // row_bricks) % col_bricks
        zb = q // (row_bricks * col_bricks)
        ys = (yb * BY + row).astype(f32)
        xs = (xb * BX + jnp.where(flip, BX - 1 - row, row)).astype(f32)
        at = pl.ds(pl.multiple_of(groups_ref[side, b] * GRP, GRP), GRP)
        freq = freq_ref[:, at]
        phase = phase_ref[:, at]
        along_x = cos_any(xs * freq[0:1] + phase[0:1])
        along_y = cos_any(ys * freq[1:2] + phase[1:2])
        along_z = cos_any(jnp.broadcast_to(zb.astype(f32) * freq[2:3] + phase[2:3], (SUB, GRP)))
        return along_x, along_y * along_z[0:1]

    pair = 2 * SUB

    def prepare(b, k):
        along_x, along_y = factors(0, b)
        xa, xb = coarse_fine(along_x)
        ya, yb = coarse_fine(along_y)
        rows_ref = rows[k]
        rows_ref[0] = xa
        rows_ref[1] = xb
        halves = []
        for h in range(BY // pair):
            at = slice(h * pair, (h + 1) * pair)
            halves.append((ya[at].astype(bf16), yb[at].astype(bf16), along_y[at].astype(bf16)))
        block = jnp.concatenate(split(stage_ref[b]), axis=1)
        block = jnp.concatenate([block, block], axis=0)
        per_part = BY * BX // pair // PARTS
        for part in range(PARTS):
            coarse, fine = [], []
            for tile in range(part * per_part, (part + 1) * per_part):
                x = tile % BX
                y_a, y_b, y_all = halves[tile // BX]
                x_a, x_b = (
                    jnp.concatenate([rows_ref[p, pl.ds(x, SUB, stride=0), :]] * 2, axis=0).astype(bf16)
                    for p in range(2)
                )
                coarse.append(x_a * y_a)
                fine.append(x_a * y_b + x_b * y_all)
            left = jnp.concatenate([jnp.concatenate(coarse, axis=0), jnp.concatenate(fine, axis=0)], axis=1)
            at = slice(part * per_part * pair, (part + 1) * per_part * pair)
            mixed[k][at, :] = jnp.dot(left, block, preferred_element_type=f32)
            yield

    def finish(b, k):
        along_x, along_y = factors(1, b)
        rows_ref = rows[k]
        rows_ref[2] = along_x
        tiles = [along_y[g * SUB : (g + 1) * SUB] for g in range(BY // SUB)]

        def row_sums(first, size):
            if size == 1:
                g, x = first // BX, first % BX
                at = slice((((g // 2) * BX + x) * 2 + g % 2) * SUB, (((g // 2) * BX + x) * 2 + g % 2 + 1) * SUB)
                value = mixed[k][at, :GRP] + mixed[k][at, GRP:]
                return value * (rows_ref[2, pl.ds(x, SUB, stride=0), :] * tiles[g])
            bit = size // 2
            one, two = row_sums(first, bit), row_sums(first + bit, bit)
            return merge(one, two, bit)

        def merge(one, two, bit):
            odd = (lane & bit) != 0
            return jnp.where(odd, two, one) + pltpu.roll(jnp.where(odd, one, two), bit, 1)

        sums = jnp.zeros((SUB, LANES), f32)
        for part in range(PARTS):
            for first in range(part * (LANES // PARTS), (part + 1) * (LANES // PARTS)):
                cells = jnp.sum(row_sums(first, 1), axis=1, keepdims=True)
                sums = jnp.where(lane == first, cells, sums)
            yield
        value = sums
        q = brick_ref[b]
        zb = q // (row_bricks * col_bricks)
        home = zb // planes
        yb = (q // row_bricks) % col_bricks
        brick = ((zb % planes) * col_bricks + yb) * column_bricks + (q % row_bricks - narrow * column_bricks)
        rank = count_ref[home]
        count_ref[home] = rank + 1
        send_ref[home, pl.ds(pl.multiple_of(rank * SUB, SUB), SUB), :] = value
        head = send_ref[home, slots * SUB :, :]
        send_ref[home, slots * SUB :, :] = jnp.where(lane == rank, brick.astype(f32), head)

    def weave(*works):
        works = list(works)
        while works:
            works = [work for work in works if next(work, works) is not works]

    fetch(0).wait()
    weave(prepare(0, 0))

    def two_blocks(i, carry):
        b = 2 * i
        fetch(b + 1).wait()
        fetch(b + 2).wait()
        weave(prepare(b + 1, 1), finish(b, 0))
        weave(prepare(b + 2, 0), finish(b + 1, 1))
        return carry

    lax.fori_loop(0, count // 2 - 1, two_blocks, 0)
    fetch(count - 1).wait()
    weave(prepare(count - 1, 1), finish(count - 2, 0))
    weave(finish(count - 1, 1))


def make_pieces(blocks, groups, bricks, freq, phase, wide_size, slots, planes):
    count = blocks.shape[0]
    assert count % 2 == 0 and count >= 2
    rows = slots * SUB + SUB
    vmem = pl.BlockSpec(memory_space=pltpu.VMEM)
    smem = pl.BlockSpec(memory_space=pltpu.SMEM)
    mixed = pltpu.VMEM((BY * BX, 2 * GRP), f32)
    return pl.pallas_call(
        functools.partial(pieces_kernel, count, slots, planes),
        in_specs=[smem, smem, pl.BlockSpec(memory_space=pl.ANY), vmem, vmem],
        out_specs=vmem,
        out_shape=pltpu.VMEM((wide_size, rows, LANES), f32),
        scratch_shapes=[
            pltpu.SMEM((wide_size,), i32),
            pltpu.VMEM((count, GRP, GRP), f32),
            pltpu.SemaphoreType.DMA((count,)),
            mixed, mixed,
            pltpu.VMEM((3, BX, GRP), f32), pltpu.VMEM((3, BX, GRP), f32),
        ],
        compiler_params=pltpu.CompilerParams(vmem_limit_bytes=VMEM_LIMIT),
        name="pieces",
    )(*map(off_chip, (groups.T, bricks, blocks, freq, phase)))


def bits_of(count):
    assert count & (count - 1) == 0
    return count.bit_length() - 1


def energy_kernel(slots, got_ref, core_ref, out_ref, codes_ref, code_ref, first_ref, valence_ref, cells_ref, sem):
    wide_size = got_ref.shape[0]
    total = wide_size * slots
    narrow_size = lax.axis_size("narrow")
    narrow = lax.axis_index("narrow")
    column_bricks = core_ref.shape[1] // BX
    column_bits = bits_of(column_bricks)
    tiles = LANES // BX
    flip = 2 * narrow < narrow_size
    lane = lax.broadcasted_iota(i32, (SUB, LANES), 1)
    sub = lax.broadcasted_iota(i32, (SUB, LANES), 0)
    group = lane // BX

    heads = []
    for w in range(0, wide_size, SUB):
        head = jnp.concatenate([got_ref[w + k, slots * SUB : slots * SUB + 1, :] for k in range(SUB)], axis=0)
        heads.append(head)
        codes_ref[w : w + SUB, :] = jnp.maximum(head, 0.0).astype(i32)
    fetch = pltpu.make_async_copy(codes_ref, code_ref, sem)
    fetch.start()

    def piece(s):
        return got_ref[s // slots, (s % slots) * SUB : (s % slots + 1) * SUB, :]

    for s in range(total):
        valence_ref[s * SUB : (s + 1) * SUB, :] = jnp.zeros((SUB, LANES), f32)
    mirror = jnp.where(flip, lane - lane % BX + (BX - 1 - lane % BX), lane)
    fetch.wait()
    bricks = [code_ref[s // slots, s % slots] for s in range(total)]
    for s in range(total - 1, -1, -1):
        first_ref[bricks[s]] = s
    for s in range(total):
        owner = first_ref[bricks[s]]
        rows = pl.ds(pl.multiple_of(owner * SUB, SUB), SUB)
        valence_ref[rows, :] = valence_ref[rows, :] + piece(s)
        mark = jnp.where(owner == s, bricks[s], -1).astype(f32)
        w = s // slots
        heads[w // SUB] = jnp.where((lane == s % slots) & (sub == w % SUB), mark, heads[w // SUB])
        column = bricks[s] & (column_bricks - 1)
        y0 = pl.multiple_of((bricks[s] >> column_bits) * BY, BY)
        lanes = pl.ds(pl.multiple_of((column >> bits_of(tiles)) * LANES, LANES), LANES)
        first = column & (tiles - 1)
        value = None
        for g in range(tiles):
            block = core_ref[pl.ds(y0 + g * SUB, SUB), lanes]
            moved = pltpu.roll(block, ((g - first) & (tiles - 1)) * BX, 1)
            value = moved if value is None else jnp.where(group == g, moved, value)
        cells_ref[s * SUB : (s + 1) * SUB, :] = jnp.take_along_axis(value, mirror, axis=1)

    def four_thirds(value):
        size = jnp.maximum(jnp.abs(value), 1e-30)
        inverse = jnp.exp2(jnp.log2(size) * (-1.0 / 3.0))
        inverse = inverse * (4.0 - size * (inverse * inverse * inverse)) * (1.0 / 3.0)
        return size * (size * (inverse * inverse))

    core = cells_ref[...]
    rho = core + valence_ref[...]
    out_ref[: total * SUB, :] = energy_coef * (four_thirds(rho) - four_thirds(core))
    for k, head in enumerate(heads):
        code = jnp.maximum(head, 0.0).astype(i32)
        column = code & (column_bricks - 1)
        placed = jnp.where(flip, code - column + (column_bricks - 1 - column), code)
        rows = slice(total * SUB + k * SUB, total * SUB + (k + 1) * SUB)
        out_ref[rows, :] = jnp.where(head < 0.0, -1.0, placed.astype(f32))


def make_energy(got, core, slots):
    wide_size = got.shape[0]
    total = wide_size * slots
    bricks = (core.shape[0] // BY) * (core.shape[1] // BX)
    vmem = pl.BlockSpec(memory_space=pltpu.VMEM)
    return pl.pallas_call(
        functools.partial(energy_kernel, slots),
        in_specs=[vmem, vmem],
        out_specs=vmem,
        out_shape=pltpu.VMEM((total * SUB + wide_size, LANES), f32),
        scratch_shapes=[
            pltpu.VMEM((wide_size, LANES), i32),
            pltpu.SMEM((wide_size, LANES), i32),
            pltpu.SMEM((bricks,), i32),
            pltpu.VMEM((total * SUB, LANES), f32),
            pltpu.VMEM((total * SUB, LANES), f32),
            pltpu.SemaphoreType.DMA,
        ],
        compiler_params=pltpu.CompilerParams(vmem_limit_bytes=VMEM_LIMIT),
        name="energy",
    )(on_chip(got), core)


def tables_kernel(wy_high, wy_low, wx_high, wx_low):
    rows_all = NY // lax.axis_size("narrow")
    narrow = lax.axis_index("narrow")
    half = rows_all // 2
    depth = NY // 2
    lane = lax.broadcasted_iota(i32, (half, LANES), 1)
    row = lax.broadcasted_iota(i32, (half, LANES), 0)
    for p in range(2):
        wave = rows_all * narrow + 2 * row + p
        base_cos, base_sin = cos_sin_turn((wave * lane) % NY, NY)
        for t in range(depth // LANES):
            jump_cos, jump_sin = cos_sin_turn((wave[:SUB] * (t * LANES)) % NY, NY)
            jump_cos = jnp.concatenate([jump_cos] * (half // SUB), axis=0)
            jump_sin = jnp.concatenate([jump_sin] * (half // SUB), axis=0)
            at = slice(t * LANES, (t + 1) * LANES)
            for part, value in (
                (0, base_cos * jump_cos - base_sin * jump_sin),
                (1, -(base_sin * jump_cos + base_cos * jump_sin)),
            ):
                rows = slice(p * rows_all + part * half, p * rows_all + (part + 1) * half)
                wy_high[rows, at], wy_low[rows, at] = split(value)
    depth = NX // 2
    lane = lax.broadcasted_iota(i32, (depth, LANES), 1)
    place = 2 * lax.broadcasted_iota(i32, (depth, LANES), 0) + 1
    base_cos, base_sin = cos_sin_turn((place * lane) % (2 * NX), 2 * NX)
    for t in range(NX // 2 // LANES):
        jump_cos, jump_sin = cos_sin_turn((place[:SUB] * (t * LANES)) % (2 * NX), 2 * NX)
        jump_cos = jnp.concatenate([jump_cos] * (depth // SUB), axis=0)
        jump_sin = jnp.concatenate([jump_sin] * (depth // SUB), axis=0)
        at = slice(t * LANES, (t + 1) * LANES)
        for part, value in (
            (0, base_cos * jump_cos - base_sin * jump_sin),
            (1, base_sin * jump_cos + base_cos * jump_sin),
        ):
            rows = slice(part * depth, (part + 1) * depth)
            wx_high[rows, at], wx_low[rows, at] = split(value)


def make_tables(narrow_size):
    rows_all = NY // narrow_size
    y_shape = pltpu.VMEM((2 * rows_all, NY // 2), bf16)
    x_shape = pltpu.VMEM((NX, NX // 2), bf16)
    vmem = pl.BlockSpec(memory_space=pltpu.VMEM)
    return pl.pallas_call(
        tables_kernel,
        out_specs=[vmem] * 4,
        out_shape=[y_shape, y_shape, x_shape, x_shape],
        compiler_params=pltpu.CompilerParams(vmem_limit_bytes=VMEM_LIMIT),
        name="tables",
    )()


def along_y(slots, columns, bricks_ref, wy_high, wy_low, scratch, out_ref):
    plane_ref, codes_ref, code_ref, sem = scratch
    wide_size = codes_ref.shape[0]
    total = wide_size * slots
    column_bits = bits_of(columns // BX)
    tiles = LANES // BX
    blocks = columns // LANES
    depth = NY + BY
    group = lax.broadcasted_iota(i32, (SUB, LANES), 1) // BX
    head = bricks_ref[total * SUB :, :]
    brick = jnp.maximum(head, 0.0).astype(i32)
    column = brick & (columns // BX - 1)
    row = (column >> bits_of(tiles)) * depth + jnp.where(head < 0.0, NY, (brick >> column_bits) * BY)
    codes_ref[...] = row * tiles + (column & (tiles - 1))
    fetch = pltpu.make_async_copy(codes_ref, code_ref, sem)
    fetch.start()
    plane_ref[...] = jnp.zeros(plane_ref.shape, f32)
    fetch.wait()
    for s in range(total):
        code = code_ref[s // slots, s % slots]
        first = code & (tiles - 1)
        row = code >> bits_of(tiles)
        value = pltpu.roll(bricks_ref[s * SUB : (s + 1) * SUB, :], first * BX, 1)
        mask = group == first
        for g in range(tiles):
            moved = value if g == 0 else pltpu.roll(value, LANES - g * BX, 1)
            rows = pl.ds(pl.multiple_of(row + g * SUB, SUB), SUB)
            pltpu.store(plane_ref.at[rows, :], moved, mask=mask)
    half = NY // 2
    rows_all = wy_high.shape[0] // 2
    upper = jnp.concatenate([plane_ref[t * depth : t * depth + half, :] for t in range(blocks)], axis=1)
    lower = jnp.concatenate([plane_ref[t * depth + half : t * depth + NY, :] for t in range(blocks)], axis=1)
    dot = functools.partial(jnp.dot, preferred_element_type=f32)
    for p in range(2):
        high, low = split(upper + lower if p == 0 else upper - lower)
        rows = slice(p * rows_all, (p + 1) * rows_all)
        table = wy_high[rows, :]
        value = dot(jnp.concatenate([table, wy_low[rows, :]], axis=0), high)
        value = value[:rows_all] + value[rows_all:] + dot(table, low)
        for part in range(2):
            for t in range(blocks):
                piece = value[part * rows_all // 2 : (part + 1) * rows_all // 2, t * LANES : (t + 1) * LANES]
                out_ref[part, t, pl.ds(p, rows_all // 2, stride=2), :] = piece


def along_y_scratch(wide_size, columns):
    return [
        pltpu.VMEM((columns // LANES * (NY + BY), LANES), f32),
        pltpu.VMEM((wide_size, LANES), i32),
        pltpu.SMEM((wide_size, LANES), i32),
        pltpu.SemaphoreType.DMA,
    ]


def y_kernel(slots, columns, bricks_ref, wy_high, wy_low, out_ref, *scratch):
    along_y(slots, columns, bricks_ref, wy_high, wy_low, scratch, out_ref)


def make_y(bricks, tables, columns, wide_size, slots):
    vmem = pl.BlockSpec(memory_space=pltpu.VMEM)
    return pl.pallas_call(
        functools.partial(y_kernel, slots, columns),
        in_specs=[vmem, vmem, vmem],
        out_specs=vmem,
        out_shape=pltpu.VMEM((2, columns // LANES, tables[0].shape[0] // 2, LANES), f32),
        scratch_shapes=along_y_scratch(wide_size, columns),
        cost_estimate=pl.CostEstimate(flops=2 * 10**9, bytes_accessed=2 * 10**6, transcendentals=0),
        compiler_params=pltpu.CompilerParams(vmem_limit_bytes=VMEM_LIMIT),
        name="along_y",
    )(on_chip(bricks), on_chip(tables[0]), on_chip(tables[1]))


def x_kernel(slots, columns, mask, first, last, *refs):
    bricks_ref, near_ref, wy_high, wy_low, wx_high, wx_low = refs[:6]
    sum_ref = None if first else refs[6]
    out_ref, far_ref = refs[6 + (not first)], refs[7 + (not first)]
    scratch = refs[8 + (not first) :]
    half_size = lax.axis_size("narrow") // 2
    narrow = lax.axis_index("narrow")
    blocks = columns // LANES
    along_y(slots, columns, bricks_ref, wy_high, wy_low, scratch, far_ref)

    def whole(ref, part):
        return jnp.concatenate([ref[part, t] for t in range(blocks)], axis=1)

    source = lax.bitwise_xor(narrow, mask)
    mirror = 2 * half_size - 1 - source
    sign = jnp.where(source < mirror, 1.0, -1.0).astype(f32)
    start = pl.multiple_of((jnp.maximum(source, mirror) - half_size) * columns, columns)
    cos_rows = pl.ds(start, columns)
    sin_rows = pl.ds(pl.multiple_of(NX // 2 + start, columns), columns)
    near = [whole(near_ref, part) for part in range(2)]
    far = [whole(far_ref, part) for part in range(2)]
    even = jnp.concatenate([a + b for a, b in zip(near, far)], axis=0)
    odd = jnp.concatenate([(far[1] - near[1]) * sign, (near[0] - far[0]) * sign], axis=0)
    even_high, even_low = split(even)
    odd_high, odd_low = split(odd)
    both = jnp.dot(
        jnp.concatenate([even_high, even_low, even_high, odd_high, odd_low, odd_high], axis=1),
        jnp.concatenate(
            [
                wx_high[cos_rows, :], wx_high[cos_rows, :], wx_low[cos_rows, :],
                wx_high[sin_rows, :], wx_high[sin_rows, :], wx_low[sin_rows, :],
            ],
            axis=0,
        ),
        preferred_element_type=f32,
    )
    rows_all = wy_high.shape[0] // 2
    u, v = both[:rows_all], both[rows_all:]
    if not first:
        u, v = u + sum_ref[0], v + sum_ref[1]
    if last:
        lane = lax.broadcasted_iota(i32, (SUB, NX // 2), 1)
        phase_cos, phase_sin = cos_sin_turn((lane * (NX - 1)) % (2 * NX), 2 * NX)
        scale = 1.0 / math.sqrt(NX * NY)
        phase_cos, phase_sin = phase_cos[0:1] * scale, phase_sin[0:1] * scale
        u, v = u * phase_cos + v * phase_sin, v * phase_cos - u * phase_sin
    out_ref[0] = u
    out_ref[1] = v


def make_x(bricks, near, mask, tables, total, last, wide_size, slots):
    first = total is None
    rows_all = tables[0].shape[0] // 2
    columns = near.shape[1] * LANES
    vmem = pl.BlockSpec(memory_space=pltpu.VMEM)
    args = (bricks, near, *tables) if first else (bricks, near, *tables, total)
    return pl.pallas_call(
        functools.partial(x_kernel, slots, columns, mask, first, last),
        in_specs=[vmem] * len(args),
        out_specs=vmem,
        out_shape=(jax.ShapeDtypeStruct if last else pltpu.VMEM)((2, rows_all, NX // 2), f32),
        scratch_shapes=[pltpu.VMEM(near.shape, f32)] + along_y_scratch(wide_size, columns),
        compiler_params=pltpu.CompilerParams(vmem_limit_bytes=VMEM_LIMIT),
        name="along_x",
    )(*map(on_chip, args))


def local(density_blocks, block_groups, block_brick, orbital_freq, orbital_phase, core_density):
    wide_size = lax.axis_size("wide")
    narrow_size = lax.axis_size("narrow")
    block_count = density_blocks.shape[0]
    slots = (2 * block_count + wide_size - 1) // wide_size
    planes, grid_rows, columns = core_density.shape
    half_size = narrow_size // 2
    assert narrow_size & (narrow_size - 1) == 0 and planes == 1 and slots <= LANES
    send = make_pieces(
        density_blocks, block_groups, block_brick, orbital_freq, orbital_phase, wide_size, slots, planes
    )
    got = lax.all_to_all(send, "wide", split_axis=0, concat_axis=0, tiled=True)
    own = make_energy(got, core_density.reshape(grid_rows, columns), slots)

    def across(value, mask):
        return lax.ppermute(value, "narrow", [(i, i ^ mask) for i in range(narrow_size)])

    bricks = {0: own}
    step = half_size
    while step:
        bricks |= {mask | step: across(value, step) for mask, value in bricks.items()}
        step //= 2
    tables = make_tables(narrow_size)
    early = [make_y(bricks[mask], tables, columns, wide_size, slots) for mask in range(half_size)]
    total = None
    for late in range(half_size, narrow_size):
        mask = narrow_size - 1 - late
        total = make_x(
            bricks[late], early[mask], mask, tables, total, late == narrow_size - 1, wide_size, slots
        )
    return total[None]


def solution(mesh):
    return jax.shard_map(
        local,
        mesh=mesh,
        in_specs=(
            P(("wide", "narrow"), None, None),
            P(("wide", "narrow"), None),
            P(("wide", "narrow")),
            P(),
            P(),
            P("wide", None, "narrow"),
        ),
        out_specs=P("wide", None, "narrow", None),
        check_vma=False,
    )
```
